256 devices in a mesh: energy: 64 (over z_hi, y, x), slab: 4 (over z_lo, core).
Axes of the slice: x: 4, y: 4, z: 8 (z_hi: 4, z_lo: 2; z = z_hi * 2 + z_lo), core: 2. Of those that a mesh axis runs over, the one named last changes fastest.
Arguments:
- g_less: bfloat16 [1024, 4, 5, 64, 128], P('energy', 'slab'), may hold values from -6 to 6
- g_greater: bfloat16 [1024, 4, 5, 64, 128], P('energy', 'slab'), may hold values from -6 to 6
- coulomb: bfloat16 [4, 64, 192], P('slab'), may hold values from -0.4375 to 0.4375
- pattern: int32 [4, 5], replicated, may hold values from 0 to 9, as said below
Outputs:
- screened: bfloat16 [1024, 4, 5, 64, 128], P('energy', 'slab')
The draws below stay inside these ranges and needn't reach their ends.
Inputs may be any that keep to these rules, and one draw needn't show every extreme that they name: `pattern`: row r holds 5 distinct columns: r, r + 3, r + 6 and two of r + 1, r + 2, r + 4, r + 5, in any order of slots.
All inputs are finite; a program needn't handle non-finite values.
Results may differ from the reference program's by a relative error of at most 0.007.
Values may be sent and summed in bfloat16 or wider, within the bound.
No kernel may reach another device: no remote copies, remote signals or barrier semaphores. Data moves between devices by JAX's collectives and lax.ppermute only.
A program may use at most 64 MiB of HBM per device.

```python
import math
import jax
import jax.numpy as jnp
from jax import lax

NE = 1024
BI = 64
SLOTS = 5
ROWS = 4


def draw_pattern(key, part):
    first_key = jax.random.fold_in(key, 11)
    second_key = jax.random.fold_in(key, 23)
    choices_table = jnp.array([1, 2, 4, 5], dtype=jnp.int32)
    scores = jax.random.randint(first_key, (ROWS, 4), 0, 4096) * 8 + jnp.arange(4, dtype=jnp.int32)[None, :]
    ranking = jnp.argsort(scores, axis=1, stable=True)
    chosen = choices_table[ranking[:, :2]]
    fixed_part = jnp.broadcast_to(jnp.array([0, 3, 6], dtype=jnp.int32)[None, :], (ROWS, 3))
    offsets = jnp.concatenate([fixed_part, chosen], 1)
    order_scores = jax.random.randint(second_key, (ROWS, 5), 0, 4096) * 8 + jnp.arange(5, dtype=jnp.int32)[None, :]
    ordering = jnp.argsort(order_scores, axis=1, stable=True)
    offsets = jnp.take_along_axis(offsets, ordering, axis=1)
    return (jnp.arange(ROWS, dtype=jnp.int32)[:, None] + offsets).astype(jnp.int32)


def block_levels(stream_key, dims, cuts, smallest, top_value):
    level, own = 1.0, jax.random.fold_in(stream_key, 6)
    for axis_at, shards_of in cuts:
        heights = jnp.exp(jax.random.uniform(jax.random.fold_in(own, axis_at), (shards_of,), jnp.float32, smallest / len(cuts), top_value / len(cuts)))
        level = level * jnp.repeat(heights, dims[axis_at] // shards_of).reshape([-1 if axis == axis_at else 1 for axis in range(len(dims))])
    return level


def bell_draw(own_key, shape, scale, bound, pieces=(), held_as=jnp.bfloat16):
    values = jax.random.normal(own_key, shape, jnp.float32) * scale
    if len(pieces) > 0:
        values = block_levels(own_key, shape, pieces, -0.22, 0.18) * values
    return jnp.clip(values, min=-bound, max=bound).astype(held_as)


def setup_inputs(seed: int = 0) -> dict:
    key_list = jax.random.split(jax.random.key(seed), 5)
    g_less = bell_draw(key_list[0], (NE, ROWS, SLOTS, BI, 2 * BI), 1.0, 6.0, ((0, 64), (1, 4)))
    g_greater = bell_draw(key_list[1], (NE, ROWS, SLOTS, BI, 2 * BI), 1.0, 6.0, ((0, 64), (1, 4)))
    coulomb = bell_draw(key_list[2], (ROWS, BI, 3 * BI), (3 * BI) ** -0.5, 0.4375, ((0, 4),))
    pattern = draw_pattern(jax.random.fold_in(key_list[4], 71), 0)
    return {"g_less": g_less, "g_greater": g_greater, "coulomb": coulomb, "pattern": pattern}


def make_tables():
    energy_index = jnp.arange(NE, dtype=jnp.int32)
    phases = energy_index[:, None] * energy_index[None, :] % NE
    angles = phases.astype(jnp.float32) * (2.0 * math.pi / NE)
    norm_scale = 1.0 / math.sqrt(NE)
    table_real = (jnp.cos(angles) * norm_scale).astype(jnp.bfloat16)
    table_imag = (-jnp.sin(angles) * norm_scale).astype(jnp.bfloat16)
    return (table_real, table_imag)

def two_products(values, table_real, table_imag):
    flat = values.reshape(NE, -1).astype(jnp.float32)
    direct = jnp.dot(table_real.astype(jnp.float32), flat, preferred_element_type=jnp.float32).reshape(values.shape)
    swapped = jnp.dot(table_imag.astype(jnp.float32), flat, preferred_element_type=jnp.float32).reshape(values.shape)
    return (direct, swapped)

def reference(g_less, g_greater, coulomb, pattern):
    table_real, table_imag = make_tables()
    half_cols = BI

    def polar_row(row_index):
        lesser = lax.dynamic_index_in_dim(g_less, row_index, 1, keepdims=False)
        greater = lax.dynamic_index_in_dim(g_greater, row_index, 1, keepdims=False)
        direct, swapped = two_products(lesser, table_real, table_imag)
        less_real = direct[..., :half_cols] - swapped[..., half_cols:]
        less_imag = direct[..., half_cols:] + swapped[..., :half_cols]
        direct, swapped = two_products(greater, table_real, table_imag)
        great_real = direct[..., :half_cols] - swapped[..., half_cols:]
        great_imag = direct[..., half_cols:] + swapped[..., :half_cols]
        prod_real = less_real * great_real + less_imag * great_imag
        prod_imag = less_imag * great_real - less_real * great_imag
        product = jnp.concatenate([prod_real, prod_imag], -1).astype(jnp.bfloat16)
        direct, swapped = two_products(product, table_real, table_imag)
        back_real = direct[..., :half_cols] + swapped[..., half_cols:]
        back_imag = direct[..., half_cols:] - swapped[..., :half_cols]
        return jnp.concatenate([back_real, back_imag], -1).astype(jnp.bfloat16)
    polar = jnp.moveaxis(lax.map(polar_row, jnp.arange(ROWS, dtype=jnp.int32)), 0, 1)
    padded = jnp.pad(polar, ((0, 0), (1, 1), (0, 0), (0, 0), (0, 0)))
    filler = jnp.full((1, SLOTS), -1, jnp.int32)
    extended = jnp.concatenate([filler, pattern.astype(jnp.int32), filler], 0)

    def screen_row(row_index):
        neighbours = lax.dynamic_slice_in_dim(padded, row_index, 3, 1).astype(jnp.float32)
        columns = lax.dynamic_slice_in_dim(extended, row_index, 3, 0)
        selector = (columns[:, None, :] == columns[1][None, :, None]).astype(jnp.float32)
        picked = jnp.einsum('dst,edtin->edsin', selector, neighbours)
        weights = lax.dynamic_index_in_dim(coulomb, row_index, 0, keepdims=False)
        weights = weights.reshape(BI, 3, BI).astype(jnp.float32)
        return jnp.einsum('adi,edsin->esan', weights, picked).astype(jnp.bfloat16)
    screened = lax.map(screen_row, jnp.arange(ROWS, dtype=jnp.int32))
    return jnp.moveaxis(screened, 0, 1)
```

```python
import functools
import math

import jax
import jax.numpy as jnp
import ml_dtypes
import numpy as np
from jax import lax
from jax.experimental import pallas as pl
from jax.experimental.pallas import tpu as pltpu
from jax.sharding import Mesh, PartitionSpec as P

NE = 1024
QUART = NE // 4
NZ = 4
NP = 16
NL = 16
ALL = ("z", "y", "x", "s")
PLANE = ("y", "x")
STEPS = (3, 1, -1, -3)


def tables():
    e = np.arange(QUART)
    out = []
    for first in range(4):
        t = 4 * np.arange(QUART) + first
        angle = 2.0 * math.pi * ((e[:, None] * t[None, :]) % NE) / NE
        scale = 1.0 / math.sqrt(NE)
        real = (np.cos(angle) * scale).astype(np.float32).astype(ml_dtypes.bfloat16)
        imag = (-np.sin(angle) * scale).astype(np.float32).astype(ml_dtypes.bfloat16)
        out.append((real, imag))
    forward = np.stack([np.concatenate([r.T, i.T], 0) for r, i in out])
    inverse = np.stack([np.concatenate([r, i], 0) for r, i in out])
    return forward, inverse


def hop(piece, step):
    perm = []
    for z in range(4):
        for yx in range(16):
            for s in range(4):
                to = (2 * z + s // 2 + step) % 8
                perm.append(((z * 16 + yx) * 4 + s, ((to // 2) * 16 + yx) * 4 + (to % 2) * 2 + s % 2))
    return lax.ppermute(piece, ALL, perm)


def times_i(v):
    lane = lax.broadcasted_iota(jnp.int32, v.shape, 1)
    return jnp.where(lane < 64, -1.0, 1.0) * pltpu.roll(v, 64, 1)


def correlate_kernel(slots, split, rot_ref, *refs):
    less_refs, great_ref, fwd_ref, inv_ref = refs[:4], refs[4], refs[5], refs[6]
    n_out = 4 if split else 1
    outs = refs[7 : 7 + n_out]
    xl_ref, xg_ref, z_ref = refs[7 + n_out :]
    f32, bf16 = jnp.float32, jnp.bfloat16

    def butterflies(get, x_ref):
        for s in range(slots):
            x0, x1, x2, x3 = (get(j, s).reshape(QUART, 128).astype(f32) for j in range(4))
            a, b, c, d = x0 + x2, x0 - x2, x1 + x3, x1 - x3
            d = times_i(d)
            for t1, v in enumerate((a + c, b - d, a - c, b + d)):
                hi = v.astype(bf16)
                x_ref[t1, 0, :, s * 128 : (s + 1) * 128] = hi
                x_ref[t1, 1, :, s * 128 : (s + 1) * 128] = (v - hi.astype(f32)).astype(bf16)

    butterflies(lambda j, s: less_refs[j][:, s], xl_ref)
    butterflies(lambda j, s: great_ref[:, j, s], xg_ref)

    @pl.loop(0, 4)
    def _(t1):
        table, back = fwd_ref[t1], inv_ref[t1]
        for s in range(0, slots, 2):
            n = min(2, slots - s)
            cols = slice(s * 128, (s + n) * 128)

            def transform(x_ref):
                y = jnp.dot(table, x_ref[t1, 0, :, cols], preferred_element_type=f32)
                y = y + jnp.dot(table, x_ref[t1, 1, :, cols], preferred_element_type=f32)
                return y

            yl, yg = transform(xl_ref), transform(xg_ref)
            prods = []
            for k in range(n):
                own = slice(k * 128, (k + 1) * 128)
                le = yl[:QUART, own] + times_i(yl[QUART:, own])
                gr = yg[:QUART, own] + times_i(yg[QUART:, own])
                m1 = le * gr
                m2 = le * pltpu.roll(gr, 64, 1)
                lane = lax.broadcasted_iota(jnp.int32, m1.shape, 1)
                prod = jnp.where(lane < 64, m1 + pltpu.roll(m1, 64, 1), m2 - pltpu.roll(m2, 64, 1))
                prods.append(prod.astype(bf16))
            prod = prods[0] if n == 1 else jnp.concatenate(prods, 1)
            zz = jnp.dot(back, prod, preferred_element_type=f32)
            for k in range(n):
                own = slice(k * 128, (k + 1) * 128)
                z_ref[t1, :, (s + k) * 128 : (s + k + 1) * 128] = zz[:QUART, own] - times_i(zz[QUART:, own])

    ca, cb, cc = rot_ref[0], rot_ref[1], rot_ref[2]
    for s in range(slots):
        z0, z1, z2, z3 = (z_ref[t, :, s * 128 : (s + 1) * 128] for t in range(4))
        u1 = ca * z1 + cb * times_i(z1)
        u3 = ca * z3 - cb * times_i(z3)
        u2 = cc * z2
        a, b, c = z0 + u2, z0 - u2, u1 + u3
        d = times_i(u1 - u3)
        for j, v in enumerate((a + c, b - d, a - c, b + d)):
            v = v.astype(bf16).reshape(NP, NL, 128)
            if split:
                outs[j][:, s] = v
            else:
                outs[0][:, j, s] = v


def correlate(rot, less, great, fwd, inv, split):
    slots = great.shape[2]
    n = slots * 128
    vmem = pl.BlockSpec(memory_space=pltpu.VMEM)
    piece = jax.ShapeDtypeStruct((NP, slots, NL, 128), jnp.bfloat16)
    whole = jax.ShapeDtypeStruct((NP, NZ, slots, NL, 128), jnp.bfloat16)
    out = pl.pallas_call(
        functools.partial(correlate_kernel, slots, split),
        out_shape=[piece] * 4 if split else [whole],
        in_specs=[pl.BlockSpec(memory_space=pltpu.SMEM)] + [vmem] * 7,
        out_specs=[vmem] * (4 if split else 1),
        scratch_shapes=[
            pltpu.VMEM((4, 2, QUART, n), jnp.bfloat16),
            pltpu.VMEM((4, 2, QUART, n), jnp.bfloat16),
            pltpu.VMEM((4, QUART, n), jnp.float32),
        ],
        compiler_params=pltpu.CompilerParams(vmem_limit_bytes=40 << 20),
        cost_estimate=pl.CostEstimate(
            flops=2 * 4 * 512 * 256 * n * 5, bytes_accessed=3 * NE * n * 2 + (2 << 20), transcendentals=0
        ),
        name="correlate",
    )(rot, *less, great, fwd, inv)
    return out if split else out[0]


def screen_kernel(at_ref, ok_ref, w_ref, up_ref, own_ref, down_ref, out_ref):
    slots = own_ref.shape[1]
    w = w_ref[...]
    for l in range(own_ref.shape[0]):
        cols = []
        for s in range(slots):
            blocks = []
            for d, ref in enumerate((up_ref, own_ref, down_ref)):
                if d == 1:
                    blocks.append(ref[l, s])
                else:
                    got = ref[l, at_ref[d, s]]
                    blocks.append(jnp.where(ok_ref[d, s] > 0, got, jnp.zeros_like(got)))
            cols.append(jnp.concatenate(blocks, 0))
        res = jnp.dot(w, jnp.concatenate(cols, 1), preferred_element_type=jnp.float32)
        for s in range(slots):
            out_ref[l, s] = res[:, s * 128 : (s + 1) * 128].astype(jnp.bfloat16)


def screen(at, ok, weights, up, own, down):
    el, slots, bi, wide = own.shape
    step = 4
    block = pl.BlockSpec((step, slots, bi, wide), lambda i: (i, 0, 0, 0))
    smem = pl.BlockSpec(memory_space=pltpu.SMEM)
    return pl.pallas_call(
        screen_kernel,
        grid=(el // step,),
        out_shape=jax.ShapeDtypeStruct(own.shape, jnp.bfloat16),
        in_specs=[smem, smem, pl.BlockSpec(weights.shape, lambda i: (0, 0)), block, block, block],
        out_specs=block,
        cost_estimate=pl.CostEstimate(
            flops=2 * el * slots * bi * 3 * bi * wide, bytes_accessed=4 * own.size * 2, transcendentals=0
        ),
        name="screen",
    )(at, ok, weights, up, own, down)


def shards(g_less, g_greater, coulomb, pattern):
    el, rows, slots, bi, wide = g_less.shape
    iz, s_row = lax.axis_index("z"), lax.axis_index("s")
    z_lo = s_row // 2
    turn = iz + z_lo + 1
    fwd, inv = (jnp.asarray(t) for t in tables())

    def piece_of(arr, j, axis, size):
        q = (turn + 4 - j) % 4
        return lax.dynamic_slice_in_dim(arr, q * size, size, axis)

    great = g_greater.reshape(el, slots, bi, wide)
    great = [hop(piece_of(great, j, 2, NP), STEPS[j]) for j in range(4)]
    less = g_less.reshape(el, slots, NZ, NP, wide).transpose(3, 2, 1, 0, 4)
    less = lax.all_to_all(less, PLANE, split_axis=0, concat_axis=0, tiled=True)
    less = [hop(piece_of(less, j, 1, 1)[:, 0], STEPS[j]) for j in range(4)]
    great = jnp.stack(great).transpose(3, 0, 2, 1, 4)
    great = lax.all_to_all(great, PLANE, split_axis=0, concat_axis=0, tiled=True)

    c = turn % 4
    rot = jnp.stack([
        jnp.where(c == 0, 1.0, jnp.where(c == 2, -1.0, 0.0)),
        jnp.where(c == 1, 1.0, jnp.where(c == 3, -1.0, 0.0)),
        jnp.where(c % 2 == 0, 1.0, -1.0),
    ]).astype(jnp.float32)

    first = 3
    lo = correlate(rot, [p[:, :first] for p in less], great[:, :, :first], fwd, inv, True)
    hi = correlate(rot, [p[:, first:] for p in less], great[:, :, first:], fwd, inv, False)
    lo = [hop(p, STEPS[j]) for j, p in enumerate(lo)]
    hi = lax.all_to_all(hi, PLANE, split_axis=0, concat_axis=0, tiled=True)
    hi = [hop(hi[:, j], STEPS[j]) for j in range(4)]
    lo = lax.all_to_all(jnp.stack(lo, 1), PLANE, split_axis=0, concat_axis=0, tiled=True)
    lo = lo.transpose(3, 2, 1, 0, 4).reshape(el, first, bi, wide)
    hi = jnp.stack(hi).transpose(3, 2, 0, 1, 4).reshape(el, slots - first, bi, wide)
    own = jnp.concatenate([lo, hi], 1)
    up = lax.ppermute(own, "s", [(0, 1), (1, 2), (2, 3)])
    down = lax.ppermute(own, "s", [(1, 0), (2, 1), (3, 2)])

    filler = jnp.full((1, slots), -1, jnp.int32)
    extended = jnp.concatenate([filler, pattern, filler], 0)
    cols = lax.dynamic_slice_in_dim(extended, s_row, 3, 0)
    same = cols[:, None, :] == cols[1][None, :, None]
    at = jnp.argmax(same, 2).astype(jnp.int32)
    ok = jnp.any(same, 2).astype(jnp.int32)

    near = (s_row + jnp.arange(3) - 1 + 4) % 4 // 2
    order = (iz + near[:, None] + 2 + jnp.arange(4)[None, :]) % 4
    pick = (order[:, :, None] == jnp.arange(4)[None, None, :]).astype(jnp.bfloat16)
    weights = jnp.einsum(
        "djq,adqp->adjp", pick, coulomb.reshape(bi, 3, NZ, NP), preferred_element_type=jnp.float32
    ).astype(jnp.bfloat16).reshape(bi, 3 * bi)
    return screen(at, ok, weights, up, own, down)[:, None]


def solution(mesh):
    fine = Mesh(mesh.devices.reshape(4, 4, 4, 4), ALL)
    energy = ("z", "y", "x")
    return jax.shard_map(
        shards,
        mesh=fine,
        in_specs=(P(energy, "s"), P(energy, "s"), P("s"), P()),
        out_specs=P(energy, "s"),
        check_vma=False,
    )
```

```python
import functools
import math

import jax
import jax.numpy as jnp
import ml_dtypes
import numpy as np
from jax import lax
from jax.experimental import pallas as pl
from jax.experimental.pallas import tpu as pltpu
from jax.sharding import Mesh, PartitionSpec as P

NE = 1024
QUART = NE // 4
NZ = 4
NP = 16
NL = 16
ALL = ("z", "y", "x", "s")
PLANE = ("y", "x")
CUT = 3
HEAVY = 100 * 10**9
STEPS = (3, 1, -1, -3)


def tables():
    e = np.arange(QUART)
    out = []
    for first in range(4):
        t = 4 * np.arange(QUART) + first
        angle = 2.0 * math.pi * ((e[:, None] * t[None, :]) % NE) / NE
        scale = 1.0 / math.sqrt(NE)
        real = (np.cos(angle) * scale).astype(np.float32).astype(ml_dtypes.bfloat16)
        imag = (-np.sin(angle) * scale).astype(np.float32).astype(ml_dtypes.bfloat16)
        out.append((real, imag))
    forward = np.stack([np.concatenate([r.T, i.T]) for r, i in out])
    inverse = np.stack([np.concatenate([r, i]) for r, i in out])
    return forward, inverse


def hop(piece, step):
    perm = []
    for z in range(4):
        for yx in range(16):
            for s in range(4):
                to = (2 * z + s // 2 + step) % 8
                perm.append(((z * 16 + yx) * 4 + s, ((to // 2) * 16 + yx) * 4 + (to % 2) * 2 + s % 2))
    return lax.ppermute(piece, ALL, perm)


def times_i(v):
    lane = lax.broadcasted_iota(jnp.int32, v.shape, 1)
    return jnp.where(lane < 64, -1.0, 1.0) * pltpu.roll(v, 64, 1)


def correlate_kernel(slots, pieces, split, rot_ref, *refs):
    in_refs, fwd_ref, inv_ref = refs[:pieces], refs[pieces], refs[pieces + 1]
    n_out = 4 if split else 1
    outs = refs[pieces + 2 : pieces + 2 + n_out]
    xl_ref, xg_ref, p_ref, y_ref, z_ref, f_ref, b_ref, sem = refs[pieces + 2 + n_out :]
    loads = [pltpu.make_async_copy(fwd_ref, f_ref, sem.at[0]), pltpu.make_async_copy(inv_ref, b_ref, sem.at[1])]
    for load in loads:
        load.start()
    f32, bf16 = jnp.float32, jnp.bfloat16
    left = lax.broadcasted_iota(jnp.int32, (32, 128), 1) < 64

    def fetch(j, which, s, p):
        ref = in_refs[j][p : p + 2, which, s] if pieces == 4 else in_refs[0][p : p + 2, j, which, s]
        return ref.reshape(2 * NL, 128).astype(f32)

    for s in range(slots):
        cols = slice(s * 128, (s + 1) * 128)
        for which, x_ref in enumerate((xl_ref, xg_ref)):
            for p in range(0, NP, 2):
                rows = slice(p * NL, (p + 2) * NL)
                x0, x1, x2, x3 = (fetch(j, which, s, p) for j in range(4))
                a, b, c, d = x0 + x2, x0 - x2, x1 + x3, times_i(x1 - x3)
                for t1, v in enumerate((a + c, b - d, a - c, b + d)):
                    hi = v.astype(bf16)
                    x_ref[t1, 0, rows, cols] = hi
                    x_ref[t1, 1, rows, cols] = (v - hi.astype(f32)).astype(bf16)

    for load in loads:
        load.wait()

    @pl.loop(0, 4)
    def _(t1):
        table, back = f_ref[t1], b_ref[t1]
        for s in range(0, slots, 2):
            n = min(2, slots - s)
            cols = slice(s * 128, (s + n) * 128)
            width = slice(0, n * 128)
            for k, x_ref in enumerate((xl_ref, xg_ref)):
                y_ref[k, :, width] = jnp.dot(table, x_ref[t1, 0, :, cols], preferred_element_type=f32) + jnp.dot(
                    table, x_ref[t1, 1, :, cols], preferred_element_type=f32
                )
            for k in range(n):
                own = slice(k * 128, (k + 1) * 128)
                for r in range(0, QUART, 32):
                    one, two = slice(r, r + 32), slice(QUART + r, QUART + r + 32)
                    le = y_ref[0, one, own] + times_i(y_ref[0, two, own])
                    gr = y_ref[1, one, own] + times_i(y_ref[1, two, own])
                    m1, m2 = le * gr, le * pltpu.roll(gr, 64, 1)
                    p_ref[one, own] = (
                        jnp.where(left, m1, m2) + pltpu.roll(jnp.where(left, -m2, m1), 64, 1)
                    ).astype(bf16)
            z_ref[t1, :, cols] = jnp.dot(back, p_ref[:, width], preferred_element_type=f32)

    ca, cb, cc = rot_ref[0], rot_ref[1], rot_ref[2]
    for s in range(slots):
        cols = slice(s * 128, (s + 1) * 128)
        for p in range(0, NP, 2):
            one = slice(p * NL, (p + 2) * NL)
            two = slice(QUART + p * NL, QUART + (p + 2) * NL)
            z0, z1, z2, z3 = (z_ref[t, one, cols] - times_i(z_ref[t, two, cols]) for t in range(4))
            u2 = cc * z2
            a, b = z0 + u2, z0 - u2
            plus, minus = z1 + z3, times_i(z1 - z3)
            c = ca * plus + cb * minus
            d = ca * minus - cb * plus
            for j, v in enumerate((a + c, b - d, a - c, b + d)):
                v = v.astype(bf16).reshape(2, NL, 128)
                if split:
                    outs[j][p : p + 2, s] = v
                else:
                    outs[0][p : p + 2, j, s] = v


def correlate(rot, inputs, fwd, inv, split):
    slots = inputs[0].shape[-3]
    n = slots * 128
    vmem = pl.BlockSpec(memory_space=pltpu.VMEM)
    hbm = pl.BlockSpec(memory_space=pltpu.HBM)
    piece = jax.ShapeDtypeStruct((NP, slots, NL, 128), jnp.bfloat16)
    whole = jax.ShapeDtypeStruct((NP, NZ, slots, NL, 128), jnp.bfloat16)
    out = pl.pallas_call(
        functools.partial(correlate_kernel, slots, len(inputs), split),
        out_shape=[piece] * 4 if split else [whole],
        in_specs=[pl.BlockSpec(memory_space=pltpu.SMEM)] + [vmem] * len(inputs) + [hbm] * 2,
        out_specs=[vmem] * (4 if split else 1),
        scratch_shapes=[
            pltpu.VMEM((4, 2, QUART, n), jnp.bfloat16),
            pltpu.VMEM((4, 2, QUART, n), jnp.bfloat16),
            pltpu.VMEM((QUART, 256), jnp.bfloat16),
            pltpu.VMEM((2, 2 * QUART, 256), jnp.float32),
            pltpu.VMEM((4, 2 * QUART, n), jnp.float32),
            pltpu.VMEM((4, 2 * QUART, QUART), jnp.bfloat16),
            pltpu.VMEM((4, 2 * QUART, QUART), jnp.bfloat16),
            pltpu.SemaphoreType.DMA((2,)),
        ],
        compiler_params=pltpu.CompilerParams(vmem_limit_bytes=40 << 20),
        cost_estimate=pl.CostEstimate(
            flops=HEAVY, bytes_accessed=3 * NE * n * 2 + (2 << 20), transcendentals=0
        ),
        name="correlate",
    )(rot, *inputs, fwd, inv)
    return out if split else out[0]


def turning():
    row = lax.broadcasted_iota(jnp.int32, (256, 256), 0)
    col = lax.broadcasted_iota(jnp.int32, (256, 256), 1)
    return jnp.where((row % 16) * 16 + row // 16 == col, 1.0, 0.0).astype(jnp.bfloat16)


def prepare_kernel(cut, turn_ref, less_ref, great_ref, *refs):
    early_ref, late_refs, turn, held, sem = refs[0], refs[1:5], refs[5], refs[6], refs[7]
    slots = less_ref.shape[1]
    loads = [
        [pltpu.make_async_copy(ref.at[:, s], held.at[s, k], sem.at[s, k]) for k, ref in enumerate((less_ref, great_ref))]
        for s in range(slots)
    ]
    order = [*range(cut, slots), *range(cut)]
    for s in order:
        for load in loads[s]:
            load.start()
    turn[...] = turning()
    for s in order:
        for load in loads[s]:
            load.wait()
        for j in range(4):
            q = lax.rem(turn_ref[0] + 4 - j, 4)
            at = pl.ds(pl.multiple_of(q * NP, NP), NP)
            x = jnp.concatenate([held[s, k, :, at, :].reshape(256, 128) for k in range(2)], 1)
            x = jnp.dot(turn[...], x, preferred_element_type=jnp.float32).astype(jnp.bfloat16)
            for k in range(2):
                v = x[:, k * 128 : (k + 1) * 128].reshape(NP, NL, 128)
                if s < cut:
                    early_ref[:, j, k, s] = v
                else:
                    late_refs[j][:, k, s - cut] = v


def prepare(turn, less, great, cut):
    el, slots, bi, wide = less.shape
    vmem = pl.BlockSpec(memory_space=pltpu.VMEM)
    hbm = pl.BlockSpec(memory_space=pltpu.HBM)
    piece = jax.ShapeDtypeStruct((NP, 2, slots - cut, el, wide), jnp.bfloat16)
    early, *late = pl.pallas_call(
        functools.partial(prepare_kernel, cut),
        out_shape=[jax.ShapeDtypeStruct((NP, NZ, 2, cut, el, wide), jnp.bfloat16)] + [piece] * 4,
        in_specs=[pl.BlockSpec(memory_space=pltpu.SMEM), hbm, hbm],
        out_specs=[vmem] * 5,
        scratch_shapes=[
            pltpu.VMEM((256, 256), jnp.bfloat16),
            pltpu.VMEM((slots, 2, el, bi, wide), jnp.bfloat16),
            pltpu.SemaphoreType.DMA((slots, 2)),
        ],
        compiler_params=pltpu.CompilerParams(vmem_limit_bytes=20 << 20),
        cost_estimate=pl.CostEstimate(flops=0, bytes_accessed=4 * el * slots * bi * wide * 2, transcendentals=0),
        name="prepare",
    )(turn, less, great)
    return early, late


def settle_kernel(slots, *refs):
    in_refs, out_ref, turn = refs[:-2], refs[-2], refs[-1]
    turn[...] = turning()
    for j in range(4):
        for s in range(slots):
            x = (in_refs[j][:, s] if len(in_refs) == 4 else in_refs[0][:, j, s]).reshape(256, 128)
            x = jnp.dot(turn[...], x, preferred_element_type=jnp.float32).astype(jnp.bfloat16)
            out_ref[:, s, j * NP : (j + 1) * NP] = x.reshape(NL, NP, 128)


def settle(inputs, flops):
    slots = inputs[0].shape[-3]
    vmem = pl.BlockSpec(memory_space=pltpu.VMEM)
    return pl.pallas_call(
        functools.partial(settle_kernel, slots),
        out_shape=jax.ShapeDtypeStruct((NL, slots, 64, 128), jnp.bfloat16),
        in_specs=[vmem] * len(inputs),
        out_specs=vmem,
        scratch_shapes=[pltpu.VMEM((256, 256), jnp.bfloat16)],
        cost_estimate=pl.CostEstimate(flops=flops, bytes_accessed=NL * slots * 64 * 128 * 4, transcendentals=0),
        name="settle",
    )(*inputs)


def gather_kernel(*refs):
    sem = refs[5]
    copies = [pltpu.make_async_copy(refs[j], refs[4].at[:, j], sem.at[j]) for j in range(4)]
    for copy in copies:
        copy.start()
    for copy in copies:
        copy.wait()


def gather(pieces, flops):
    shape = pieces[0].shape
    hbm = pl.BlockSpec(memory_space=pltpu.HBM)
    return pl.pallas_call(
        gather_kernel,
        out_shape=jax.ShapeDtypeStruct((shape[0], 4, *shape[1:]), jnp.bfloat16),
        in_specs=[hbm] * 4,
        out_specs=hbm,
        scratch_shapes=[pltpu.SemaphoreType.DMA((4,))],
        cost_estimate=pl.CostEstimate(flops=flops, bytes_accessed=8 * pieces[0].size * 2, transcendentals=0),
        name="gather",
    )(*pieces)


def screen_kernel(row_ref, pattern_ref, w_ref, up_ref, own_ref, down_ref, out_ref):
    slots = own_ref.shape[1]
    rows = pattern_ref.shape[0]
    row = row_ref[0]
    found = {}
    for d, step in ((0, -1), (2, 1)):
        k = row + step
        inside = jnp.logical_and(k >= 0, k < rows)
        k = jnp.clip(k, 0, rows - 1)
        for s in range(slots):
            want = pattern_ref[row, s]
            at, hit = jnp.int32(0), jnp.int32(0)
            for t in range(slots):
                same = jnp.logical_and(inside, pattern_ref[k, t] == want)
                at = jnp.where(same, t, at)
                hit = jnp.where(same, 1, hit)
            found[d, s] = at, hit
    w = w_ref[...]
    for l in range(own_ref.shape[0]):
        cols = []
        for s in range(slots):
            blocks = []
            for d, ref in enumerate((up_ref, own_ref, down_ref)):
                if d == 1:
                    blocks.append(ref[l, s])
                else:
                    at, hit = found[d, s]
                    got = ref[l, at]
                    blocks.append(jnp.where(hit > 0, got, jnp.zeros_like(got)))
            cols.append(jnp.concatenate(blocks, 0))
        res = jnp.dot(w, jnp.concatenate(cols, 1), preferred_element_type=jnp.float32)
        for s in range(slots):
            out_ref[l, s] = res[:, s * 128 : (s + 1) * 128].astype(jnp.bfloat16)


def screen(row, pattern, weights, up, own, down):
    el, slots, bi, wide = own.shape
    step = 4
    block = pl.BlockSpec((step, slots, bi, wide), lambda i: (i, 0, 0, 0))
    smem = pl.BlockSpec(memory_space=pltpu.SMEM)
    return pl.pallas_call(
        screen_kernel,
        grid=(el // step,),
        out_shape=jax.ShapeDtypeStruct(own.shape, jnp.bfloat16),
        in_specs=[smem, smem, pl.BlockSpec(weights.shape, lambda i: (0, 0)), block, block, block],
        out_specs=block,
        cost_estimate=pl.CostEstimate(
            flops=2 * el * slots * bi * 3 * bi * wide, bytes_accessed=4 * own.size * 2, transcendentals=0
        ),
        name="screen",
    )(row, pattern, weights, up, own, down)


def shards(g_less, g_greater, coulomb, pattern):
    el, rows, slots, bi, wide = g_less.shape
    iz, s_row = lax.axis_index("z"), lax.axis_index("s")
    z_lo = s_row // 2
    turn = iz + z_lo + 1
    fwd, inv = (jnp.asarray(t) for t in tables())

    def piece_of(arr, j, axis, size):
        q = (turn + 4 - j) % 4
        return lax.dynamic_slice_in_dim(arr, q * size, size, axis)

    c = turn % 4
    rot = jnp.stack([
        jnp.where(c == 0, 1.0, jnp.where(c == 2, -1.0, 0.0)),
        jnp.where(c == 1, 1.0, jnp.where(c == 3, -1.0, 0.0)),
        jnp.where(c % 2 == 0, 1.0, -1.0),
    ]).astype(jnp.float32)
    near = (s_row + jnp.arange(3) - 1 + 4) % 4 // 2
    order = (iz + near[:, None] + 2 + jnp.arange(4)[None, :]) % 4
    pick = (order[:, :, None] == jnp.arange(4)[None, None, :]).astype(jnp.bfloat16)
    weights = jnp.einsum(
        "djq,adqp->adjp", pick, coulomb.reshape(bi, 3, NZ, NP), preferred_element_type=jnp.float32
    ).astype(jnp.bfloat16).reshape(bi, 3 * bi)

    cut = CUT
    both = (g_less.reshape(el, slots, bi, wide), g_greater.reshape(el, slots, bi, wide))
    early, late = prepare((turn % 4).reshape(1), *both, cut)
    late = gather([hop(late[j], STEPS[j]) for j in range(4)], HEAVY)
    early = lax.all_to_all(early, PLANE, split_axis=0, concat_axis=0, tiled=True)
    early = lax.optimization_barrier([early, late])[0]
    early = [hop(early[:, j], STEPS[j]) for j in range(4)]
    late = lax.all_to_all(late, PLANE, split_axis=0, concat_axis=0, tiled=True)

    lo = correlate(rot, early, fwd, inv, True)
    late = lax.optimization_barrier([late] + list(lo))[0]
    hi = correlate(rot, [late], fwd, inv, False)

    lo = gather([hop(p, STEPS[j]) for j, p in enumerate(lo)], HEAVY)
    hi = lax.all_to_all(hi, PLANE, split_axis=0, concat_axis=0, tiled=True)
    hi = lax.optimization_barrier([hi, lo])[0]
    hi = settle([hop(hi[:, j], STEPS[j]) for j in range(4)], HEAVY)
    lo = lax.all_to_all(lo, PLANE, split_axis=0, concat_axis=0, tiled=True)
    lo = settle([lax.optimization_barrier([lo, hi])[0]], 0)
    own = jnp.concatenate([lo, hi], 1)
    up = lax.ppermute(own, "s", [(0, 1), (1, 2), (2, 3)])
    down = lax.ppermute(own, "s", [(1, 0), (2, 1), (3, 2)])
    return screen(s_row.reshape(1), pattern, weights, up, own, down)[:, None]


def solution(mesh):
    fine = Mesh(mesh.devices.reshape(4, 4, 4, 4), ALL)
    energy = ("z", "y", "x")
    return jax.shard_map(
        shards,
        mesh=fine,
        in_specs=(P(energy, "s"), P(energy, "s"), P("s"), P()),
        out_specs=P(energy, "s"),
        check_vma=False,
    )
```

```python
import functools
import math

import jax
import jax.numpy as jnp
import ml_dtypes
import numpy as np
from jax import lax
from jax.experimental import pallas as pl
from jax.experimental.pallas import tpu as pltpu
from jax.sharding import Mesh, PartitionSpec as P

NE = 1024
QUART = NE // 4
NZ = 4
NP = 16
NL = 16
ALL = ("z", "y", "x", "s")
PLANE = ("y", "x")
CUT = 3
BUF = 2
HEAVY = 100 * 10**9
STEPS = (3, 1, -1, -3)


def tables():
    e = np.arange(QUART)
    out = []
    for first in range(4):
        t = 4 * np.arange(QUART) + first
        angle = 2.0 * math.pi * ((e[:, None] * t[None, :]) % NE) / NE
        scale = 1.0 / math.sqrt(NE)
        real = (np.cos(angle) * scale).astype(np.float32).astype(ml_dtypes.bfloat16)
        imag = (-np.sin(angle) * scale).astype(np.float32).astype(ml_dtypes.bfloat16)
        out.append((real, imag))
    forward = np.stack([np.concatenate([r.T, i.T]) for r, i in out])
    inverse = np.stack([np.concatenate([r, i]) for r, i in out])
    return forward, inverse


def hop(piece, step):
    perm = []
    for z in range(4):
        for yx in range(16):
            for s in range(4):
                to = (2 * z + s // 2 + step) % 8
                perm.append(((z * 16 + yx) * 4 + s, ((to // 2) * 16 + yx) * 4 + (to % 2) * 2 + s % 2))
    return lax.ppermute(piece, ALL, perm)


def times_i(v):
    lane = lax.broadcasted_iota(jnp.int32, v.shape, 1)
    return jnp.where(lane < 64, -1.0, 1.0) * pltpu.roll(v, 64, 1)


def correlate_kernel(slots, pieces, split, rot_ref, *refs):
    in_refs, fwd_ref, inv_ref = refs[:pieces], refs[pieces], refs[pieces + 1]
    n_out = 4 if split else 1
    outs = refs[pieces + 2 : pieces + 2 + n_out]
    x_ref, p_ref, y_ref, z_ref, f_ref, b_ref, sem = refs[pieces + 2 + n_out :]
    loads = [
        [pltpu.make_async_copy(ref.at[t1], held.at[t1], sem.at[k, t1]) for t1 in range(4)]
        for k, (ref, held) in enumerate(((fwd_ref, f_ref), (inv_ref, b_ref)))
    ]
    for t1 in range(4):
        for k in range(2):
            loads[k][t1].start()
    f32, bf16 = jnp.float32, jnp.bfloat16
    left = lax.broadcasted_iota(jnp.int32, (32, 128), 1) < 64

    def fetch(j, which, s, p):
        ref = in_refs[j][p : p + 2, which, s] if pieces == 4 else in_refs[0][p : p + 2, j, which, s]
        return ref.reshape(2 * NL, 128).astype(f32)

    for s in range(slots):
        for which in range(2):
            cols = slice((which * slots + s) * 128, (which * slots + s + 1) * 128)
            for p in range(0, NP, 2):
                rows = slice(p * NL, (p + 2) * NL)
                x0, x1, x2, x3 = (fetch(j, which, s, p) for j in range(4))
                a, b, c, d = x0 + x2, x0 - x2, x1 + x3, times_i(x1 - x3)
                for t1, v in enumerate((a + c, b - d, a - c, b + d)):
                    hi = v.astype(bf16)
                    x_ref[t1, 0, rows, cols] = hi
                    x_ref[t1, 1, rows, cols] = (v - hi.astype(f32)).astype(bf16)

    n = slots * 128
    for t1 in range(4):
        loads[0][t1].wait()
        loads[1][t1].wait()
        table, at = f_ref[t1], t1 % BUF
        y_ref[at] = jnp.dot(table, x_ref[t1, 0], preferred_element_type=f32) + jnp.dot(
            table, x_ref[t1, 1], preferred_element_type=f32
        )
        for s in range(slots):
            own, other = slice(s * 128, (s + 1) * 128), slice(n + s * 128, n + (s + 1) * 128)
            for r in range(0, QUART, 32):
                one, two = slice(r, r + 32), slice(QUART + r, QUART + r + 32)
                le = y_ref[at, one, own] + times_i(y_ref[at, two, own])
                gr = y_ref[at, one, other] + times_i(y_ref[at, two, other])
                m1, m2 = le * gr, le * pltpu.roll(gr, 64, 1)
                p_ref[at, one, own] = (
                    jnp.where(left, m1, m2) + pltpu.roll(jnp.where(left, -m2, m1), 64, 1)
                ).astype(bf16)
        z_ref[t1] = jnp.dot(b_ref[t1], p_ref[at], preferred_element_type=f32)

    ca, cb, cc = rot_ref[0], rot_ref[1], rot_ref[2]
    for s in range(slots):
        cols = slice(s * 128, (s + 1) * 128)
        for p in range(0, NP, 2):
            one = slice(p * NL, (p + 2) * NL)
            two = slice(QUART + p * NL, QUART + (p + 2) * NL)
            z0, z1, z2, z3 = (z_ref[t, one, cols] - times_i(z_ref[t, two, cols]) for t in range(4))
            u2 = cc * z2
            a, b = z0 + u2, z0 - u2
            plus, minus = z1 + z3, times_i(z1 - z3)
            c = ca * plus + cb * minus
            d = ca * minus - cb * plus
            for j, v in enumerate((a + c, b - d, a - c, b + d)):
                v = v.astype(bf16).reshape(2, NL, 128)
                if split:
                    outs[j][p : p + 2, s] = v
                else:
                    outs[0][p : p + 2, j, s] = v


def correlate(rot, inputs, fwd, inv, split):
    slots = inputs[0].shape[-3]
    n = slots * 128
    vmem = pl.BlockSpec(memory_space=pltpu.VMEM)
    hbm = pl.BlockSpec(memory_space=pltpu.HBM)
    piece = jax.ShapeDtypeStruct((NP, slots, NL, 128), jnp.bfloat16)
    whole = jax.ShapeDtypeStruct((NP, NZ, slots, NL, 128), jnp.bfloat16)
    out = pl.pallas_call(
        functools.partial(correlate_kernel, slots, len(inputs), split),
        out_shape=[piece] * 4 if split else [whole],
        in_specs=[pl.BlockSpec(memory_space=pltpu.SMEM)] + [vmem] * len(inputs) + [hbm] * 2,
        out_specs=[vmem] * (4 if split else 1),
        scratch_shapes=[
            pltpu.VMEM((4, 2, QUART, 2 * n), jnp.bfloat16),
            pltpu.VMEM((BUF, QUART, n), jnp.bfloat16),
            pltpu.VMEM((BUF, 2 * QUART, 2 * n), jnp.float32),
            pltpu.VMEM((4, 2 * QUART, n), jnp.float32),
            pltpu.VMEM((4, 2 * QUART, QUART), jnp.bfloat16),
            pltpu.VMEM((4, 2 * QUART, QUART), jnp.bfloat16),
            pltpu.SemaphoreType.DMA((2, 4)),
        ],
        compiler_params=pltpu.CompilerParams(vmem_limit_bytes=53 << 20),
        cost_estimate=pl.CostEstimate(
            flops=HEAVY, bytes_accessed=3 * NE * n * 2 + (2 << 20), transcendentals=0
        ),
        name="correlate",
    )(rot, *inputs, fwd, inv)
    return out if split else out[0]


def turning():
    row = lax.broadcasted_iota(jnp.int32, (256, 256), 0)
    col = lax.broadcasted_iota(jnp.int32, (256, 256), 1)
    return jnp.where((row % 16) * 16 + row // 16 == col, 1.0, 0.0).astype(jnp.bfloat16)


def prepare_kernel(cut, turn_ref, less_ref, great_ref, *refs):
    early_ref, late_refs, turn, held, sem = refs[0], refs[1:5], refs[5], refs[6], refs[7]
    slots = less_ref.shape[1]
    loads = [
        [pltpu.make_async_copy(ref.at[:, s], held.at[s, k], sem.at[s, k]) for k, ref in enumerate((less_ref, great_ref))]
        for s in range(slots)
    ]
    order = [*range(cut, slots), *range(cut)]
    for s in order:
        for load in loads[s]:
            load.start()
    turn[...] = turning()
    for s in order:
        for load in loads[s]:
            load.wait()
        for j in range(4):
            q = lax.rem(turn_ref[0] + 4 - j, 4)
            at = pl.ds(pl.multiple_of(q * NP, NP), NP)
            x = jnp.concatenate([held[s, k, :, at, :].reshape(256, 128) for k in range(2)], 1)
            x = jnp.dot(turn[...], x, preferred_element_type=jnp.float32).astype(jnp.bfloat16)
            for k in range(2):
                v = x[:, k * 128 : (k + 1) * 128].reshape(NP, NL, 128)
                if s < cut:
                    early_ref[:, j, k, s] = v
                else:
                    late_refs[j][:, k, s - cut] = v


def prepare(turn, less, great, cut):
    el, slots, bi, wide = less.shape
    vmem = pl.BlockSpec(memory_space=pltpu.VMEM)
    hbm = pl.BlockSpec(memory_space=pltpu.HBM)
    piece = jax.ShapeDtypeStruct((NP, 2, slots - cut, el, wide), jnp.bfloat16)
    early, *late = pl.pallas_call(
        functools.partial(prepare_kernel, cut),
        out_shape=[jax.ShapeDtypeStruct((NP, NZ, 2, cut, el, wide), jnp.bfloat16)] + [piece] * 4,
        in_specs=[pl.BlockSpec(memory_space=pltpu.SMEM), hbm, hbm],
        out_specs=[vmem] * 5,
        scratch_shapes=[
            pltpu.VMEM((256, 256), jnp.bfloat16),
            pltpu.VMEM((slots, 2, el, bi, wide), jnp.bfloat16),
            pltpu.SemaphoreType.DMA((slots, 2)),
        ],
        compiler_params=pltpu.CompilerParams(vmem_limit_bytes=60 << 20),
        cost_estimate=pl.CostEstimate(flops=0, bytes_accessed=4 * el * slots * bi * wide * 2, transcendentals=0),
        name="prepare",
    )(turn, less, great)
    return early, late


def settle_kernel(slots, pieces, *refs):
    in_refs, more, out_ref, turn = refs[:pieces], refs[pieces:-2], refs[-2], refs[-1]
    turn[...] = turning()
    for j in range(4):
        x = [(in_refs[j][:, s] if pieces == 4 else in_refs[0][:, j, s]).reshape(256, 128) for s in range(slots)]
        x = jnp.dot(turn[...], jnp.concatenate(x, 1), preferred_element_type=jnp.float32).astype(jnp.bfloat16)
        for s in range(slots):
            out_ref[:, s, j * NP : (j + 1) * NP] = x[:, s * 128 : (s + 1) * 128].reshape(NL, NP, 128)
    for ref in more:
        out_ref[:, slots:] = ref[...]


def settle(inputs, more, flops):
    slots = inputs[0].shape[-3]
    total = slots + sum(m.shape[1] for m in more)
    vmem = pl.BlockSpec(memory_space=pltpu.VMEM)
    return pl.pallas_call(
        functools.partial(settle_kernel, slots, len(inputs)),
        out_shape=jax.ShapeDtypeStruct((NL, total, 64, 128), jnp.bfloat16),
        in_specs=[vmem] * (len(inputs) + len(more)),
        out_specs=vmem,
        scratch_shapes=[pltpu.VMEM((256, 256), jnp.bfloat16)],
        cost_estimate=pl.CostEstimate(flops=flops, bytes_accessed=NL * total * 64 * 128 * 4, transcendentals=0),
        compiler_params=pltpu.CompilerParams(vmem_limit_bytes=12 << 20),
        name="settle",
    )(*inputs, *more)


def gather_kernel(*refs):
    for j in range(4):
        refs[4][:, j] = refs[j][...]


def gather(pieces, flops):
    shape = pieces[0].shape
    vmem = pl.BlockSpec(memory_space=pltpu.VMEM)
    return pl.pallas_call(
        gather_kernel,
        out_shape=jax.ShapeDtypeStruct((shape[0], 4, *shape[1:]), jnp.bfloat16),
        in_specs=[vmem] * 4,
        out_specs=vmem,
        cost_estimate=pl.CostEstimate(flops=flops, bytes_accessed=8 * pieces[0].size * 2, transcendentals=0),
        compiler_params=pltpu.CompilerParams(vmem_limit_bytes=12 << 20),
        name="gather",
    )(*pieces)


def screen_kernel(row_ref, pattern_ref, w_ref, up_ref, own_ref, down_ref, out_ref):
    slots = own_ref.shape[1]
    rows = pattern_ref.shape[0]
    row = row_ref[0]
    found = {}
    for d, step in ((0, -1), (2, 1)):
        k = row + step
        inside = jnp.logical_and(k >= 0, k < rows)
        k = jnp.clip(k, 0, rows - 1)
        for s in range(slots):
            want = pattern_ref[row, s]
            at, hit = jnp.int32(0), jnp.int32(0)
            for t in range(slots):
                same = jnp.logical_and(inside, pattern_ref[k, t] == want)
                at = jnp.where(same, t, at)
                hit = jnp.where(same, 1, hit)
            found[d, s] = at, hit
    w = w_ref[...]
    for l in range(own_ref.shape[0]):
        cols = []
        for s in range(slots):
            blocks = []
            for d, ref in enumerate((up_ref, own_ref, down_ref)):
                if d == 1:
                    blocks.append(ref[l, s])
                else:
                    at, hit = found[d, s]
                    got = ref[l, at]
                    blocks.append(jnp.where(hit > 0, got, jnp.zeros_like(got)))
            cols.append(jnp.concatenate(blocks, 0))
        res = jnp.dot(w, jnp.concatenate(cols, 1), preferred_element_type=jnp.float32)
        for s in range(slots):
            out_ref[l, s] = res[:, s * 128 : (s + 1) * 128].astype(jnp.bfloat16)


def screen(row, pattern, weights, up, own, down):
    el, slots, bi, wide = own.shape
    step = 4
    block = pl.BlockSpec((step, slots, bi, wide), lambda i: (i, 0, 0, 0))
    smem = pl.BlockSpec(memory_space=pltpu.SMEM)
    return pl.pallas_call(
        screen_kernel,
        grid=(el // step,),
        out_shape=jax.ShapeDtypeStruct(own.shape, jnp.bfloat16),
        in_specs=[smem, smem, pl.BlockSpec(weights.shape, lambda i: (0, 0)), block, block, block],
        out_specs=block,
        cost_estimate=pl.CostEstimate(
            flops=2 * el * slots * bi * 3 * bi * wide, bytes_accessed=4 * own.size * 2, transcendentals=0
        ),
        compiler_params=pltpu.CompilerParams(vmem_limit_bytes=12 << 20),
        name="screen",
    )(row, pattern, weights, up, own, down)


def shards(g_less, g_greater, coulomb, pattern):
    el, rows, slots, bi, wide = g_less.shape
    iz, s_row = lax.axis_index("z"), lax.axis_index("s")
    z_lo = s_row // 2
    turn = iz + z_lo + 1
    fwd, inv = (jnp.asarray(t) for t in tables())

    def piece_of(arr, j, axis, size):
        q = (turn + 4 - j) % 4
        return lax.dynamic_slice_in_dim(arr, q * size, size, axis)

    c = turn % 4
    rot = jnp.stack([
        jnp.where(c == 0, 1.0, jnp.where(c == 2, -1.0, 0.0)),
        jnp.where(c == 1, 1.0, jnp.where(c == 3, -1.0, 0.0)),
        jnp.where(c % 2 == 0, 1.0, -1.0),
    ]).astype(jnp.float32)
    near = (s_row + jnp.arange(3) - 1 + 4) % 4 // 2
    order = (iz + near[:, None] + 2 + jnp.arange(4)[None, :]) % 4
    pick = (order[:, :, None] == jnp.arange(4)[None, None, :]).astype(jnp.bfloat16)
    weights = jnp.einsum(
        "djq,adqp->adjp", pick, coulomb.reshape(bi, 3, NZ, NP), preferred_element_type=jnp.float32
    ).astype(jnp.bfloat16).reshape(bi, 3 * bi)

    cut = CUT
    both = (g_less.reshape(el, slots, bi, wide), g_greater.reshape(el, slots, bi, wide))
    early, late = prepare((turn % 4).reshape(1), *both, cut)
    late = gather([hop(late[j], STEPS[j]) for j in range(4)], HEAVY)
    early = lax.all_to_all(early, PLANE, split_axis=0, concat_axis=0, tiled=True)
    early = lax.optimization_barrier([early, late])[0]
    early = [hop(early[:, j], STEPS[j]) for j in range(4)]
    late = lax.all_to_all(late, PLANE, split_axis=0, concat_axis=0, tiled=True)

    lo = correlate(rot, early, fwd, inv, True)
    late = lax.optimization_barrier([late] + list(lo))[0]
    hi = correlate(rot, [late], fwd, inv, False)

    lo = gather([hop(p, STEPS[j]) for j, p in enumerate(lo)], HEAVY)
    hi = lax.all_to_all(hi, PLANE, split_axis=0, concat_axis=0, tiled=True)
    hi = lax.optimization_barrier([hi, lo])[0]
    hi = settle([hop(hi[:, j], STEPS[j]) for j in range(4)], [], HEAVY)
    lo = lax.all_to_all(lo, PLANE, split_axis=0, concat_axis=0, tiled=True)
    own = settle([lo], [hi], 0)
    up = lax.ppermute(own, "s", [(0, 1), (1, 2), (2, 3)])
    down = lax.ppermute(own, "s", [(1, 0), (2, 1), (3, 2)])
    return screen(s_row.reshape(1), pattern, weights, up, own, down)[:, None]


def solution(mesh):
    fine = Mesh(mesh.devices.reshape(4, 4, 4, 4), ALL)
    energy = ("z", "y", "x")
    return jax.shard_map(
        shards,
        mesh=fine,
        in_specs=(P(energy, "s"), P(energy, "s"), P("s"), P()),
        out_specs=P(energy, "s"),
        check_vma=False,
    )
```

```python
import functools
import math

import jax
import jax.numpy as jnp
import ml_dtypes
import numpy as np
from jax import lax
from jax.experimental import pallas as pl
from jax.experimental.pallas import tpu as pltpu
from jax.sharding import Mesh, PartitionSpec as P

NE = 1024
QUART = NE // 4
NZ = 4
NP = 16
NL = 16
ALL = ("z", "y", "x", "s")
PLANE = ("y", "x")
CUT = 3
BUF = 2
HEAVY = 100 * 10**9
STEPS = (3, 1, -1, -3)


def tables():
    e = np.arange(QUART)
    out = []
    for first in range(4):
        t = 4 * np.arange(QUART) + first
        angle = 2.0 * math.pi * ((e[:, None] * t[None, :]) % NE) / NE
        scale = 1.0 / math.sqrt(NE)
        real = (np.cos(angle) * scale).astype(np.float32).astype(ml_dtypes.bfloat16)
        imag = (-np.sin(angle) * scale).astype(np.float32).astype(ml_dtypes.bfloat16)
        out.append((real, imag))
    forward = np.stack([np.concatenate([r.T, i.T]) for r, i in out])
    inverse = np.stack([np.concatenate([r, i]) for r, i in out])
    return forward, inverse


def after(value, other):
    return lax.optimization_barrier([value, other])[0]


def hop(piece, step):
    perm = []
    for z in range(4):
        for yx in range(16):
            for s in range(4):
                to = (2 * z + s // 2 + step) % 8
                perm.append(((z * 16 + yx) * 4 + s, ((to // 2) * 16 + yx) * 4 + (to % 2) * 2 + s % 2))
    return lax.ppermute(piece, ALL, perm)


def times_i(v):
    lane = lax.broadcasted_iota(jnp.int32, v.shape, 1)
    return jnp.where(lane < 64, -1.0, 1.0) * pltpu.roll(v, 64, 1)


def correlate_kernel(slots, pieces, split, rot_ref, *refs):
    in_refs, fwd_ref, inv_ref = refs[:pieces], refs[pieces], refs[pieces + 1]
    n_out = 4 if split else 1
    outs = refs[pieces + 2 : pieces + 2 + n_out]
    x_ref, p_ref, y_ref, z_ref, f_ref, b_ref, sem = refs[pieces + 2 + n_out :]
    loads = [
        [pltpu.make_async_copy(ref.at[t1], held.at[t1], sem.at[k, t1]) for t1 in range(4)]
        for k, (ref, held) in enumerate(((fwd_ref, f_ref), (inv_ref, b_ref)))
    ]
    for t1 in range(4):
        for k in range(2):
            loads[k][t1].start()
    f32, bf16 = jnp.float32, jnp.bfloat16
    left = lax.broadcasted_iota(jnp.int32, (32, 128), 1) < 64

    def fetch(j, which, s, p):
        ref = in_refs[j][p : p + 2, which, s] if pieces == 4 else in_refs[0][p : p + 2, j, which, s]
        return ref.reshape(2 * NL, 128).astype(f32)

    for s in range(slots):
        for which in range(2):
            cols = slice((which * slots + s) * 128, (which * slots + s + 1) * 128)
            for p in range(0, NP, 2):
                rows = slice(p * NL, (p + 2) * NL)
                x0, x1, x2, x3 = (fetch(j, which, s, p) for j in range(4))
                a, b, c, d = x0 + x2, x0 - x2, x1 + x3, times_i(x1 - x3)
                for t1, v in enumerate((a + c, b - d, a - c, b + d)):
                    hi = v.astype(bf16)
                    x_ref[t1, 0, rows, cols] = hi
                    x_ref[t1, 1, rows, cols] = (v - hi.astype(f32)).astype(bf16)

    n = slots * 128
    for t1 in range(4):
        loads[0][t1].wait()
        loads[1][t1].wait()
        table, at = f_ref[t1], t1 % BUF
        y_ref[at] = jnp.dot(table, x_ref[t1, 0], preferred_element_type=f32) + jnp.dot(
            table, x_ref[t1, 1], preferred_element_type=f32
        )
        for s in range(slots):
            own, other = slice(s * 128, (s + 1) * 128), slice(n + s * 128, n + (s + 1) * 128)
            for r in range(0, QUART, 32):
                one, two = slice(r, r + 32), slice(QUART + r, QUART + r + 32)
                le = y_ref[at, one, own] + times_i(y_ref[at, two, own])
                gr = y_ref[at, one, other] + times_i(y_ref[at, two, other])
                m1, m2 = le * gr, le * pltpu.roll(gr, 64, 1)
                p_ref[at, one, own] = (
                    jnp.where(left, m1, m2) + pltpu.roll(jnp.where(left, -m2, m1), 64, 1)
                ).astype(bf16)
        z_ref[t1] = jnp.dot(b_ref[t1], p_ref[at], preferred_element_type=f32)

    ca, cb, cc = rot_ref[0], rot_ref[1], rot_ref[2]
    for s in range(slots):
        cols = slice(s * 128, (s + 1) * 128)
        for p in range(0, NP, 2):
            one = slice(p * NL, (p + 2) * NL)
            two = slice(QUART + p * NL, QUART + (p + 2) * NL)
            z0, z1, z2, z3 = (z_ref[t, one, cols] - times_i(z_ref[t, two, cols]) for t in range(4))
            u2 = cc * z2
            a, b = z0 + u2, z0 - u2
            plus, minus = z1 + z3, times_i(z1 - z3)
            c = ca * plus + cb * minus
            d = ca * minus - cb * plus
            for j, v in enumerate((a + c, b - d, a - c, b + d)):
                v = v.astype(bf16).reshape(2, NL, 128)
                if split:
                    outs[j][p : p + 2, s] = v
                else:
                    outs[0][p : p + 2, j, s] = v


def correlate(rot, inputs, fwd, inv, split, flops):
    slots = inputs[0].shape[-3]
    n = slots * 128
    vmem = pl.BlockSpec(memory_space=pltpu.VMEM)
    hbm = pl.BlockSpec(memory_space=pltpu.HBM)
    piece = jax.ShapeDtypeStruct((NP, slots, NL, 128), jnp.bfloat16)
    whole = jax.ShapeDtypeStruct((NP, NZ, slots, NL, 128), jnp.bfloat16)
    out = pl.pallas_call(
        functools.partial(correlate_kernel, slots, len(inputs), split),
        out_shape=[piece] * 4 if split else [whole],
        in_specs=[pl.BlockSpec(memory_space=pltpu.SMEM)] + [vmem] * len(inputs) + [hbm] * 2,
        out_specs=[vmem] * (4 if split else 1),
        scratch_shapes=[
            pltpu.VMEM((4, 2, QUART, 2 * n), jnp.bfloat16),
            pltpu.VMEM((BUF, QUART, n), jnp.bfloat16),
            pltpu.VMEM((BUF, 2 * QUART, 2 * n), jnp.float32),
            pltpu.VMEM((4, 2 * QUART, n), jnp.float32),
            pltpu.VMEM((4, 2 * QUART, QUART), jnp.bfloat16),
            pltpu.VMEM((4, 2 * QUART, QUART), jnp.bfloat16),
            pltpu.SemaphoreType.DMA((2, 4)),
        ],
        compiler_params=pltpu.CompilerParams(vmem_limit_bytes=52 << 20),
        cost_estimate=pl.CostEstimate(
            flops=flops, bytes_accessed=3 * NE * n * 2 + (2 << 20), transcendentals=0
        ),
        name="correlate",
    )(rot, *inputs, fwd, inv)
    return out if split else out[0]


def turning():
    row = lax.broadcasted_iota(jnp.int32, (256, 256), 0)
    col = lax.broadcasted_iota(jnp.int32, (256, 256), 1)
    return jnp.where((row % 16) * 16 + row // 16 == col, 1.0, 0.0).astype(jnp.bfloat16)


def prepare_kernel(cut, turn_ref, less_ref, great_ref, *refs):
    early_ref, late_refs, turn, held, sem = refs[0], refs[1:5], refs[5], refs[6], refs[7]
    slots = less_ref.shape[1]
    loads = [
        [pltpu.make_async_copy(ref.at[:, s], held.at[s, k], sem.at[s, k]) for k, ref in enumerate((less_ref, great_ref))]
        for s in range(slots)
    ]
    order = [*range(cut, slots), *range(cut)]
    for s in order:
        for load in loads[s]:
            load.start()
    turn[...] = turning()
    for s in order:
        for load in loads[s]:
            load.wait()
        for j in range(4):
            q = lax.rem(turn_ref[0] + 4 - j, 4)
            at = pl.ds(pl.multiple_of(q * NP, NP), NP)
            x = jnp.concatenate([held[s, k, :, at, :].reshape(256, 128) for k in range(2)], 1)
            x = jnp.dot(turn[...], x, preferred_element_type=jnp.float32).astype(jnp.bfloat16)
            for k in range(2):
                v = x[:, k * 128 : (k + 1) * 128].reshape(NP, NL, 128)
                if s < cut:
                    early_ref[:, j, k, s] = v
                else:
                    late_refs[j][:, k, s - cut] = v


def prepare(turn, less, great, cut):
    el, slots, bi, wide = less.shape
    vmem = pl.BlockSpec(memory_space=pltpu.VMEM)
    hbm = pl.BlockSpec(memory_space=pltpu.HBM)
    piece = jax.ShapeDtypeStruct((NP, 2, slots - cut, el, wide), jnp.bfloat16)
    early, *late = pl.pallas_call(
        functools.partial(prepare_kernel, cut),
        out_shape=[jax.ShapeDtypeStruct((NP, NZ, 2, cut, el, wide), jnp.bfloat16)] + [piece] * 4,
        in_specs=[pl.BlockSpec(memory_space=pltpu.SMEM), hbm, hbm],
        out_specs=[vmem] * 5,
        scratch_shapes=[
            pltpu.VMEM((256, 256), jnp.bfloat16),
            pltpu.VMEM((slots, 2, el, bi, wide), jnp.bfloat16),
            pltpu.SemaphoreType.DMA((slots, 2)),
        ],
        compiler_params=pltpu.CompilerParams(vmem_limit_bytes=60 << 20),
        cost_estimate=pl.CostEstimate(flops=0, bytes_accessed=4 * el * slots * bi * wide * 2, transcendentals=0),
        name="prepare",
    )(turn, less, great)
    return early, late


def settle_kernel(slots, pieces, *refs):
    in_refs, more, out_ref, turn = refs[:pieces], refs[pieces:-2], refs[-2], refs[-1]
    turn[...] = turning()
    for j in range(4):
        x = [(in_refs[j][:, s] if pieces == 4 else in_refs[0][:, j, s]).reshape(256, 128) for s in range(slots)]
        x = jnp.dot(turn[...], jnp.concatenate(x, 1), preferred_element_type=jnp.float32).astype(jnp.bfloat16)
        for s in range(slots):
            out_ref[:, s, j * NP : (j + 1) * NP] = x[:, s * 128 : (s + 1) * 128].reshape(NL, NP, 128)
    for ref in more:
        out_ref[:, slots:] = ref[...]


def settle(inputs, more, flops):
    slots = inputs[0].shape[-3]
    total = slots + sum(m.shape[1] for m in more)
    vmem = pl.BlockSpec(memory_space=pltpu.VMEM)
    return pl.pallas_call(
        functools.partial(settle_kernel, slots, len(inputs)),
        out_shape=jax.ShapeDtypeStruct((NL, total, 64, 128), jnp.bfloat16),
        in_specs=[vmem] * (len(inputs) + len(more)),
        out_specs=vmem,
        scratch_shapes=[pltpu.VMEM((256, 256), jnp.bfloat16)],
        cost_estimate=pl.CostEstimate(flops=flops, bytes_accessed=NL * total * 64 * 128 * 4, transcendentals=0),
        compiler_params=pltpu.CompilerParams(vmem_limit_bytes=12 << 20),
        name="settle",
    )(*inputs, *more)


def gather_kernel(*refs):
    for j in range(4):
        refs[4][:, j] = refs[j][...]


def gather(pieces, flops):
    shape = pieces[0].shape
    vmem = pl.BlockSpec(memory_space=pltpu.VMEM)
    return pl.pallas_call(
        gather_kernel,
        out_shape=jax.ShapeDtypeStruct((shape[0], 4, *shape[1:]), jnp.bfloat16),
        in_specs=[vmem] * 4,
        out_specs=vmem,
        cost_estimate=pl.CostEstimate(flops=flops, bytes_accessed=8 * pieces[0].size * 2, transcendentals=0),
        compiler_params=pltpu.CompilerParams(vmem_limit_bytes=12 << 20),
        name="gather",
    )(*pieces)


def marker(value, pieces, flops):
    hbm = pl.BlockSpec(memory_space=pl.ANY)

    def kernel(*refs):
        refs[-1][...] = refs[0][...]

    return pl.pallas_call(
        kernel,
        out_shape=jax.ShapeDtypeStruct(value.shape, value.dtype),
        in_specs=[pl.BlockSpec(memory_space=pltpu.VMEM)] + [hbm] * len(pieces),
        out_specs=pl.BlockSpec(memory_space=pltpu.VMEM),
        cost_estimate=pl.CostEstimate(flops=flops, bytes_accessed=4096, transcendentals=0),
        compiler_params=pltpu.CompilerParams(vmem_limit_bytes=1 << 20),
        name="marker",
    )(value, *pieces)


def screen_kernel(row_ref, pattern_ref, w_ref, up_ref, own_ref, down_ref, out_ref):
    slots = own_ref.shape[1]
    rows = pattern_ref.shape[0]
    row = row_ref[0]
    found = {}
    for d, step in ((0, -1), (2, 1)):
        k = row + step
        inside = jnp.logical_and(k >= 0, k < rows)
        k = jnp.clip(k, 0, rows - 1)
        for s in range(slots):
            want = pattern_ref[row, s]
            at, hit = jnp.int32(0), jnp.int32(0)
            for t in range(slots):
                same = jnp.logical_and(inside, pattern_ref[k, t] == want)
                at = jnp.where(same, t, at)
                hit = jnp.where(same, 1, hit)
            found[d, s] = at, hit
    w = w_ref[...]
    for l in range(own_ref.shape[0]):
        cols = []
        for s in range(slots):
            blocks = []
            for d, ref in enumerate((up_ref, own_ref, down_ref)):
                if d == 1:
                    blocks.append(ref[l, s])
                else:
                    at, hit = found[d, s]
                    got = ref[l, at]
                    blocks.append(jnp.where(hit > 0, got, jnp.zeros_like(got)))
            cols.append(jnp.concatenate(blocks, 0))
        res = jnp.dot(w, jnp.concatenate(cols, 1), preferred_element_type=jnp.float32)
        for s in range(slots):
            out_ref[l, s] = res[:, s * 128 : (s + 1) * 128].astype(jnp.bfloat16)


def screen(row, pattern, weights, up, own, down):
    el, slots, bi, wide = own.shape
    step = 4
    block = pl.BlockSpec((step, slots, bi, wide), lambda i: (i, 0, 0, 0))
    smem = pl.BlockSpec(memory_space=pltpu.SMEM)
    return pl.pallas_call(
        screen_kernel,
        grid=(el // step,),
        out_shape=jax.ShapeDtypeStruct(own.shape, jnp.bfloat16),
        in_specs=[smem, smem, pl.BlockSpec(weights.shape, lambda i: (0, 0)), block, block, block],
        out_specs=block,
        cost_estimate=pl.CostEstimate(
            flops=2 * el * slots * bi * 3 * bi * wide, bytes_accessed=4 * own.size * 2, transcendentals=0
        ),
        compiler_params=pltpu.CompilerParams(vmem_limit_bytes=12 << 20),
        name="screen",
    )(row, pattern, weights, up, own, down)


def shards(g_less, g_greater, coulomb, pattern):
    el, rows, slots, bi, wide = g_less.shape
    iz, s_row = lax.axis_index("z"), lax.axis_index("s")
    z_lo = s_row // 2
    turn = iz + z_lo + 1
    fwd, inv = (jnp.asarray(t) for t in tables())

    def piece_of(arr, j, axis, size):
        q = (turn + 4 - j) % 4
        return lax.dynamic_slice_in_dim(arr, q * size, size, axis)

    c = turn % 4
    rot = jnp.stack([
        jnp.where(c == 0, 1.0, jnp.where(c == 2, -1.0, 0.0)),
        jnp.where(c == 1, 1.0, jnp.where(c == 3, -1.0, 0.0)),
        jnp.where(c % 2 == 0, 1.0, -1.0),
    ]).astype(jnp.float32)
    near = (s_row + jnp.arange(3) - 1 + 4) % 4 // 2
    order = (iz + near[:, None] + 2 + jnp.arange(4)[None, :]) % 4
    pick = (order[:, :, None] == jnp.arange(4)[None, None, :]).astype(jnp.bfloat16)
    weights = jnp.einsum(
        "djq,adqp->adjp", pick, coulomb.reshape(bi, 3, NZ, NP), preferred_element_type=jnp.float32
    ).astype(jnp.bfloat16).reshape(bi, 3 * bi)

    cut = CUT
    both = (g_less.reshape(el, slots, bi, wide), g_greater.reshape(el, slots, bi, wide))
    early, late = prepare((turn % 4).reshape(1), *both, cut)
    late = gather([hop(late[j], STEPS[j]) for j in range(4)], HEAVY)
    early = lax.all_to_all(early, PLANE, split_axis=0, concat_axis=0, tiled=True)
    early = after(early, late)
    early = [hop(early[:, j], STEPS[j]) for j in range(4)]
    late = lax.all_to_all(late, PLANE, split_axis=0, concat_axis=0, tiled=True)

    late, rot = lax.optimization_barrier([late, marker(rot, early[1:3], HEAVY)])
    hi = correlate(rot, [late], fwd, inv, True, 0)
    early[0] = after(early[0], hi[0])
    lo = correlate(rot, early, fwd, inv, True, HEAVY)

    hi = gather([hop(p, STEPS[j]) for j, p in enumerate(hi)], 0)
    hi = lax.all_to_all(hi, PLANE, split_axis=0, concat_axis=0, tiled=True)
    lo = gather([hop(p, STEPS[j]) for j, p in enumerate(lo)], HEAVY)
    hi = settle([after(hi, lo)], [], 0)
    lo = lax.all_to_all(lo, PLANE, split_axis=0, concat_axis=0, tiled=True)
    own = settle([lo], [hi], 0)
    up = lax.ppermute(own, "s", [(0, 1), (1, 2), (2, 3)])
    down = lax.ppermute(own, "s", [(1, 0), (2, 1), (3, 2)])
    return screen(s_row.reshape(1), pattern, weights, up, own, down)[:, None]


def solution(mesh):
    fine = Mesh(mesh.devices.reshape(4, 4, 4, 4), ALL)
    energy = ("z", "y", "x")
    return jax.shard_map(
        shards,
        mesh=fine,
        in_specs=(P(energy, "s"), P(energy, "s"), P("s"), P()),
        out_specs=P(energy, "s"),
        check_vma=False,
    )
```

```python
import functools
import math

import jax
import jax.numpy as jnp
import ml_dtypes
import numpy as np
from jax import lax
from jax.experimental import pallas as pl
from jax.experimental.pallas import tpu as pltpu
from jax.sharding import Mesh, PartitionSpec as P

NE = 1024
QUART = NE // 4
NZ = 4
NP = 16
NL = 16
ALL = ("z", "y", "x", "s")
PLANE = ("y", "x")
CUT = 3
BUF = 2
HEAVY = 100 * 10**9
STEPS = (3, 1, -1, -3)


def tables():
    e = np.arange(QUART)
    out = []
    for first in range(4):
        t = 4 * np.arange(QUART) + first
        angle = 2.0 * math.pi * ((e[:, None] * t[None, :]) % NE) / NE
        scale = 1.0 / math.sqrt(NE)
        real = (np.cos(angle) * scale).astype(np.float32).astype(ml_dtypes.bfloat16)
        imag = (-np.sin(angle) * scale).astype(np.float32).astype(ml_dtypes.bfloat16)
        out.append((real, imag))
    forward = np.stack([np.concatenate([r.T, i.T]) for r, i in out])
    inverse = np.stack([np.concatenate([r, i]) for r, i in out])
    return forward, inverse


def after(value, other):
    return lax.optimization_barrier([value, other])[0]


def hop(piece, step):
    perm = []
    for z in range(4):
        for yx in range(16):
            for s in range(4):
                to = (2 * z + s // 2 + step) % 8
                perm.append(((z * 16 + yx) * 4 + s, ((to // 2) * 16 + yx) * 4 + (to % 2) * 2 + s % 2))
    return lax.ppermute(piece, ALL, perm)


def times_i(v):
    lane = lax.broadcasted_iota(jnp.int32, v.shape, 1)
    return jnp.where(lane < 64, -1.0, 1.0) * pltpu.roll(v, 64, 1)


def correlate_kernel(slots, pieces, split, rot_ref, *refs):
    in_refs, fwd_ref, inv_ref = refs[:pieces], refs[pieces], refs[pieces + 1]
    n_out = 4 if split else 1
    outs = refs[pieces + 2 : pieces + 2 + n_out]
    x_ref, p_ref, y_ref, z_ref, f_ref, b_ref, sem = refs[pieces + 2 + n_out :]
    loads = [
        [pltpu.make_async_copy(ref.at[t1], held.at[t1], sem.at[k, t1]) for t1 in range(4)]
        for k, (ref, held) in enumerate(((fwd_ref, f_ref), (inv_ref, b_ref)))
    ]
    for t1 in range(4):
        for k in range(2):
            loads[k][t1].start()
    f32, bf16 = jnp.float32, jnp.bfloat16
    left = lax.broadcasted_iota(jnp.int32, (32, 128), 1) < 64

    def fetch(j, which, s, p):
        ref = in_refs[j][p : p + 2, which, s] if pieces == 4 else in_refs[0][p : p + 2, j, which, s]
        return ref.reshape(2 * NL, 128).astype(f32)

    for s in range(slots):
        for which in range(2):
            cols = slice((which * slots + s) * 128, (which * slots + s + 1) * 128)
            for p in range(0, NP, 2):
                rows = slice(p * NL, (p + 2) * NL)
                x0, x1, x2, x3 = (fetch(j, which, s, p) for j in range(4))
                a, b, c, d = x0 + x2, x0 - x2, x1 + x3, times_i(x1 - x3)
                for t1, v in enumerate((a + c, b - d, a - c, b + d)):
                    hi = v.astype(bf16)
                    x_ref[t1, 0, rows, cols] = hi
                    x_ref[t1, 1, rows, cols] = (v - hi.astype(f32)).astype(bf16)

    n = slots * 128
    for t1 in range(4):
        loads[0][t1].wait()
        loads[1][t1].wait()
        table, at = f_ref[t1], t1 % BUF
        y_ref[at] = jnp.dot(table, x_ref[t1, 0], preferred_element_type=f32) + jnp.dot(
            table, x_ref[t1, 1], preferred_element_type=f32
        )
        for s in range(slots):
            own, other = slice(s * 128, (s + 1) * 128), slice(n + s * 128, n + (s + 1) * 128)
            for r in range(0, QUART, 32):
                one, two = slice(r, r + 32), slice(QUART + r, QUART + r + 32)
                le = y_ref[at, one, own] + times_i(y_ref[at, two, own])
                gr = y_ref[at, one, other] + times_i(y_ref[at, two, other])
                m1, m2 = le * gr, le * pltpu.roll(gr, 64, 1)
                p_ref[at, one, own] = (
                    jnp.where(left, m1, m2) + pltpu.roll(jnp.where(left, -m2, m1), 64, 1)
                ).astype(bf16)
        z_ref[t1] = jnp.dot(b_ref[t1], p_ref[at], preferred_element_type=f32)

    ca, cb, cc = rot_ref[0], rot_ref[1], rot_ref[2]
    for s in range(slots):
        cols = slice(s * 128, (s + 1) * 128)
        for p in range(0, NP, 2):
            one = slice(p * NL, (p + 2) * NL)
            two = slice(QUART + p * NL, QUART + (p + 2) * NL)
            z0, z1, z2, z3 = (z_ref[t, one, cols] - times_i(z_ref[t, two, cols]) for t in range(4))
            u2 = cc * z2
            a, b = z0 + u2, z0 - u2
            plus, minus = z1 + z3, times_i(z1 - z3)
            c = ca * plus + cb * minus
            d = ca * minus - cb * plus
            for j, v in enumerate((a + c, b - d, a - c, b + d)):
                v = v.astype(bf16).reshape(2, NL, 128)
                if split:
                    outs[j][p : p + 2, s] = v
                else:
                    outs[0][p : p + 2, j, s] = v


def correlate(rot, inputs, fwd, inv, split, flops):
    slots = inputs[0].shape[-3]
    n = slots * 128
    vmem = pl.BlockSpec(memory_space=pltpu.VMEM)
    hbm = pl.BlockSpec(memory_space=pltpu.HBM)
    piece = jax.ShapeDtypeStruct((NP, slots, NL, 128), jnp.bfloat16)
    whole = jax.ShapeDtypeStruct((NP, NZ, slots, NL, 128), jnp.bfloat16)
    out = pl.pallas_call(
        functools.partial(correlate_kernel, slots, len(inputs), split),
        out_shape=[piece] * 4 if split else [whole],
        in_specs=[pl.BlockSpec(memory_space=pltpu.SMEM)] + [vmem] * len(inputs) + [hbm] * 2,
        out_specs=[vmem] * (4 if split else 1),
        scratch_shapes=[
            pltpu.VMEM((4, 2, QUART, 2 * n), jnp.bfloat16),
            pltpu.VMEM((BUF, QUART, n), jnp.bfloat16),
            pltpu.VMEM((BUF, 2 * QUART, 2 * n), jnp.float32),
            pltpu.VMEM((4, 2 * QUART, n), jnp.float32),
            pltpu.VMEM((4, 2 * QUART, QUART), jnp.bfloat16),
            pltpu.VMEM((4, 2 * QUART, QUART), jnp.bfloat16),
            pltpu.SemaphoreType.DMA((2, 4)),
        ],
        compiler_params=pltpu.CompilerParams(vmem_limit_bytes=52 << 20),
        cost_estimate=pl.CostEstimate(
            flops=flops, bytes_accessed=3 * NE * n * 2 + (2 << 20), transcendentals=0
        ),
        name="correlate",
    )(rot, *inputs, fwd, inv)
    return out if split else out[0]


def turning():
    row = lax.broadcasted_iota(jnp.int32, (256, 256), 0)
    col = lax.broadcasted_iota(jnp.int32, (256, 256), 1)
    return jnp.where((row % 16) * 16 + row // 16 == col, 1.0, 0.0).astype(jnp.bfloat16)


def prepare_kernel(cut, turn_ref, less_ref, great_ref, *refs):
    early_ref, late_refs, turn, held, sem = refs[0], refs[1:5], refs[5], refs[6], refs[7]
    slots = less_ref.shape[1]
    loads = [
        [pltpu.make_async_copy(ref.at[:, s], held.at[s, k], sem.at[s, k]) for k, ref in enumerate((less_ref, great_ref))]
        for s in range(slots)
    ]
    order = [*range(cut, slots), *range(cut)]
    for s in order:
        for load in loads[s]:
            load.start()
    turn[...] = turning()
    for s in order:
        for load in loads[s]:
            load.wait()
        for j in range(4):
            q = lax.rem(turn_ref[0] + 4 - j, 4)
            at = pl.ds(pl.multiple_of(q * NP, NP), NP)
            x = jnp.concatenate([held[s, k, :, at, :].reshape(256, 128) for k in range(2)], 1)
            x = jnp.dot(turn[...], x, preferred_element_type=jnp.float32).astype(jnp.bfloat16)
            for k in range(2):
                v = x[:, k * 128 : (k + 1) * 128].reshape(NP, NL, 128)
                if s < cut:
                    early_ref[:, j, k, s] = v
                else:
                    late_refs[j][:, k, s - cut] = v


def prepare(turn, less, great, cut):
    el, slots, bi, wide = less.shape
    vmem = pl.BlockSpec(memory_space=pltpu.VMEM)
    hbm = pl.BlockSpec(memory_space=pltpu.HBM)
    piece = jax.ShapeDtypeStruct((NP, 2, slots - cut, el, wide), jnp.bfloat16)
    early, *late = pl.pallas_call(
        functools.partial(prepare_kernel, cut),
        out_shape=[jax.ShapeDtypeStruct((NP, NZ, 2, cut, el, wide), jnp.bfloat16)] + [piece] * 4,
        in_specs=[pl.BlockSpec(memory_space=pltpu.SMEM), hbm, hbm],
        out_specs=[vmem] * 5,
        scratch_shapes=[
            pltpu.VMEM((256, 256), jnp.bfloat16),
            pltpu.VMEM((slots, 2, el, bi, wide), jnp.bfloat16),
            pltpu.SemaphoreType.DMA((slots, 2)),
        ],
        compiler_params=pltpu.CompilerParams(vmem_limit_bytes=60 << 20),
        cost_estimate=pl.CostEstimate(flops=0, bytes_accessed=4 * el * slots * bi * wide * 2, transcendentals=0),
        name="prepare",
    )(turn, less, great)
    return early, late


def settle_kernel(slots, pieces, *refs):
    in_refs, more, out_ref, turn = refs[:pieces], refs[pieces:-2], refs[-2], refs[-1]
    turn[...] = turning()
    for j in range(4):
        x = [(in_refs[j][:, s] if pieces == 4 else in_refs[0][:, j, s]).reshape(256, 128) for s in range(slots)]
        x = jnp.dot(turn[...], jnp.concatenate(x, 1), preferred_element_type=jnp.float32).astype(jnp.bfloat16)
        for s in range(slots):
            out_ref[:, s, j * NP : (j + 1) * NP] = x[:, s * 128 : (s + 1) * 128].reshape(NL, NP, 128)
    for ref in more:
        out_ref[:, slots:] = ref[...]


def settle(inputs, more, flops):
    slots = inputs[0].shape[-3]
    total = slots + sum(m.shape[1] for m in more)
    vmem = pl.BlockSpec(memory_space=pltpu.VMEM)
    return pl.pallas_call(
        functools.partial(settle_kernel, slots, len(inputs)),
        out_shape=jax.ShapeDtypeStruct((NL, total, 64, 128), jnp.bfloat16),
        in_specs=[vmem] * (len(inputs) + len(more)),
        out_specs=vmem,
        scratch_shapes=[pltpu.VMEM((256, 256), jnp.bfloat16)],
        cost_estimate=pl.CostEstimate(flops=flops, bytes_accessed=NL * total * 64 * 128 * 4, transcendentals=0),
        compiler_params=pltpu.CompilerParams(vmem_limit_bytes=12 << 20),
        name="settle",
    )(*inputs, *more)


def gather_kernel(*refs):
    for j in range(4):
        refs[4][:, j] = refs[j][...]


def gather(pieces, flops):
    shape = pieces[0].shape
    vmem = pl.BlockSpec(memory_space=pltpu.VMEM)
    return pl.pallas_call(
        gather_kernel,
        out_shape=jax.ShapeDtypeStruct((shape[0], 4, *shape[1:]), jnp.bfloat16),
        in_specs=[vmem] * 4,
        out_specs=vmem,
        cost_estimate=pl.CostEstimate(flops=flops, bytes_accessed=8 * pieces[0].size * 2, transcendentals=0),
        compiler_params=pltpu.CompilerParams(vmem_limit_bytes=12 << 20),
        name="gather",
    )(*pieces)


def marker(value, pieces, flops):
    hbm = pl.BlockSpec(memory_space=pl.ANY)

    def kernel(*refs):
        refs[-1][...] = refs[0][...]

    return pl.pallas_call(
        kernel,
        out_shape=jax.ShapeDtypeStruct(value.shape, value.dtype),
        in_specs=[pl.BlockSpec(memory_space=pltpu.VMEM)] + [hbm] * len(pieces),
        out_specs=pl.BlockSpec(memory_space=pltpu.VMEM),
        cost_estimate=pl.CostEstimate(flops=flops, bytes_accessed=4096, transcendentals=0),
        compiler_params=pltpu.CompilerParams(vmem_limit_bytes=1 << 20),
        name="marker",
    )(value, *pieces)


def screen_kernel(row_ref, pattern_ref, w_ref, up_ref, own_ref, down_ref, out_ref):
    slots = own_ref.shape[1]
    rows = pattern_ref.shape[0]
    row = row_ref[0]
    found = {}
    for d, step in ((0, -1), (2, 1)):
        k = row + step
        inside = jnp.logical_and(k >= 0, k < rows)
        k = jnp.clip(k, 0, rows - 1)
        for s in range(slots):
            want = pattern_ref[row, s]
            at, hit = jnp.int32(0), jnp.int32(0)
            for t in range(slots):
                same = jnp.logical_and(inside, pattern_ref[k, t] == want)
                at = jnp.where(same, t, at)
                hit = jnp.where(same, 1, hit)
            found[d, s] = at, hit
    w = w_ref[...]
    for l in range(own_ref.shape[0]):
        cols = []
        for s in range(slots):
            blocks = []
            for d, ref in enumerate((up_ref, own_ref, down_ref)):
                if d == 1:
                    blocks.append(ref[l, s])
                else:
                    at, hit = found[d, s]
                    got = ref[l, at]
                    blocks.append(jnp.where(hit > 0, got, jnp.zeros_like(got)))
            cols.append(jnp.concatenate(blocks, 0))
        res = jnp.dot(w, jnp.concatenate(cols, 1), preferred_element_type=jnp.float32)
        for s in range(slots):
            out_ref[l, s] = res[:, s * 128 : (s + 1) * 128].astype(jnp.bfloat16)


def screen(row, pattern, weights, up, own, down):
    el, slots, bi, wide = own.shape
    step = 4
    block = pl.BlockSpec((step, slots, bi, wide), lambda i: (i, 0, 0, 0))
    smem = pl.BlockSpec(memory_space=pltpu.SMEM)
    return pl.pallas_call(
        screen_kernel,
        grid=(el // step,),
        out_shape=jax.ShapeDtypeStruct(own.shape, jnp.bfloat16),
        in_specs=[smem, smem, pl.BlockSpec(weights.shape, lambda i: (0, 0)), block, block, block],
        out_specs=block,
        cost_estimate=pl.CostEstimate(
            flops=2 * el * slots * bi * 3 * bi * wide, bytes_accessed=4 * own.size * 2, transcendentals=0
        ),
        compiler_params=pltpu.CompilerParams(vmem_limit_bytes=12 << 20),
        name="screen",
    )(row, pattern, weights, up, own, down)


def shards(g_less, g_greater, coulomb, pattern):
    el, rows, slots, bi, wide = g_less.shape
    iz, s_row = lax.axis_index("z"), lax.axis_index("s")
    z_lo = s_row // 2
    turn = iz + z_lo + 1
    fwd, inv = (jnp.asarray(t) for t in tables())

    def piece_of(arr, j, axis, size):
        q = (turn + 4 - j) % 4
        return lax.dynamic_slice_in_dim(arr, q * size, size, axis)

    c = turn % 4
    rot = jnp.stack([
        jnp.where(c == 0, 1.0, jnp.where(c == 2, -1.0, 0.0)),
        jnp.where(c == 1, 1.0, jnp.where(c == 3, -1.0, 0.0)),
        jnp.where(c % 2 == 0, 1.0, -1.0),
    ]).astype(jnp.float32)
    near = (s_row + jnp.arange(3) - 1 + 4) % 4 // 2
    order = (iz + near[:, None] + 2 + jnp.arange(4)[None, :]) % 4
    pick = (order[:, :, None] == jnp.arange(4)[None, None, :]).astype(jnp.bfloat16)
    weights = jnp.einsum(
        "djq,adqp->adjp", pick, coulomb.reshape(bi, 3, NZ, NP), preferred_element_type=jnp.float32
    ).astype(jnp.bfloat16).reshape(bi, 3 * bi)

    cut = CUT
    both = (g_less.reshape(el, slots, bi, wide), g_greater.reshape(el, slots, bi, wide))
    early, late = prepare((turn % 4).reshape(1), *both, cut)
    late = gather([hop(late[j], STEPS[j]) for j in range(4)], HEAVY)
    early = lax.all_to_all(early, PLANE, split_axis=0, concat_axis=0, tiled=True)
    early = after(early, late)
    early = [hop(early[:, j], STEPS[j]) for j in range(4)]
    late = lax.all_to_all(late, PLANE, split_axis=0, concat_axis=0, tiled=True)

    late, rot = lax.optimization_barrier([late, marker(rot, early[1:3], HEAVY)])
    hi = correlate(rot, [late], fwd, inv, False, 0)
    early[0] = after(early[0], hi)
    lo = correlate(rot, early, fwd, inv, True, HEAVY)

    hi = lax.all_to_all(hi, PLANE, split_axis=0, concat_axis=0, tiled=True)
    lo = gather([hop(p, STEPS[j]) for j, p in enumerate(lo)], 0)
    hi = settle([hop(hi[:, j], STEPS[j]) for j in range(4)], [], 0)
    lo = lax.all_to_all(lo, PLANE, split_axis=0, concat_axis=0, tiled=True)
    own = settle([lo], [hi], 0)
    up = lax.ppermute(own, "s", [(0, 1), (1, 2), (2, 3)])
    down = lax.ppermute(own, "s", [(1, 0), (2, 1), (3, 2)])
    return screen(s_row.reshape(1), pattern, weights, up, own, down)[:, None]


def solution(mesh):
    fine = Mesh(mesh.devices.reshape(4, 4, 4, 4), ALL)
    energy = ("z", "y", "x")
    return jax.shard_map(
        shards,
        mesh=fine,
        in_specs=(P(energy, "s"), P(energy, "s"), P("s"), P()),
        out_specs=P(energy, "s"),
        check_vma=False,
    )
```

```python
import functools
import math

import jax
import jax.numpy as jnp
import ml_dtypes
import numpy as np
from jax import lax
from jax.experimental import pallas as pl
from jax.experimental.pallas import tpu as pltpu
from jax.sharding import Mesh, PartitionSpec as P

NE = 1024
QUART = NE // 4
NZ = 4
NP = 16
NL = 16
ALL = ("z", "y", "x", "s")
PLANE = ("y", "x")
CUT = 3
ORDER = (0, 3, 1, 2)
BUF = 2
HEAVY = 100 * 10**9
STEPS = (3, 1, -1, -3)


def tables():
    e = np.arange(QUART)
    out = []
    for first in range(4):
        t = 4 * np.arange(QUART) + first
        angle = 2.0 * math.pi * ((e[:, None] * t[None, :]) % NE) / NE
        scale = 1.0 / math.sqrt(NE)
        real = (np.cos(angle) * scale).astype(np.float32).astype(ml_dtypes.bfloat16)
        imag = (-np.sin(angle) * scale).astype(np.float32).astype(ml_dtypes.bfloat16)
        out.append((real, imag))
    forward = np.stack([np.concatenate([r.T, i.T]) for r, i in out])
    inverse = np.stack([np.concatenate([r, i]) for r, i in out])
    return forward, inverse


def after(value, other):
    return lax.optimization_barrier([value, other])[0]


def hop(piece, step):
    perm = []
    for z in range(4):
        for yx in range(16):
            for s in range(4):
                to = (2 * z + s // 2 + step) % 8
                perm.append(((z * 16 + yx) * 4 + s, ((to // 2) * 16 + yx) * 4 + (to % 2) * 2 + s % 2))
    return lax.ppermute(piece, ALL, perm)


def times_i(v):
    lane = lax.broadcasted_iota(jnp.int32, v.shape, 1)
    return jnp.where(lane < 64, -1.0, 1.0) * pltpu.roll(v, 64, 1)


def correlate_kernel(slots, pieces, split, rot_ref, *refs):
    in_refs, fwd_ref, inv_ref = refs[:pieces], refs[pieces], refs[pieces + 1]
    n_out = 4 if split else 1
    outs = refs[pieces + 2 : pieces + 2 + n_out]
    x_ref, p_ref, y_ref, z_ref, f_ref, b_ref, sem = refs[pieces + 2 + n_out :]
    loads = [
        [pltpu.make_async_copy(ref.at[t1], held.at[t1], sem.at[k, t1]) for t1 in range(4)]
        for k, (ref, held) in enumerate(((fwd_ref, f_ref), (inv_ref, b_ref)))
    ]
    for t1 in range(4):
        for k in range(2):
            loads[k][t1].start()
    f32, bf16 = jnp.float32, jnp.bfloat16
    left = lax.broadcasted_iota(jnp.int32, (32, 128), 1) < 64

    def fetch(j, which, s, p):
        ref = in_refs[j][p : p + 2, which, s] if pieces == 4 else in_refs[0][p : p + 2, j, which, s]
        return ref.reshape(2 * NL, 128).astype(f32)

    for s in range(slots):
        for which in range(2):
            cols = slice((which * slots + s) * 128, (which * slots + s + 1) * 128)
            for p in range(0, NP, 2):
                rows = slice(p * NL, (p + 2) * NL)
                x0, x1, x2, x3 = (fetch(j, which, s, p) for j in range(4))
                a, b, c, d = x0 + x2, x0 - x2, x1 + x3, times_i(x1 - x3)
                for t1, v in enumerate((a + c, b - d, a - c, b + d)):
                    hi = v.astype(bf16)
                    x_ref[t1, 0, rows, cols] = hi
                    x_ref[t1, 1, rows, cols] = (v - hi.astype(f32)).astype(bf16)

    n = slots * 128
    for t1 in range(4):
        loads[0][t1].wait()
        loads[1][t1].wait()
        table, at = f_ref[t1], t1 % BUF
        y_ref[at] = jnp.dot(table, x_ref[t1, 0], preferred_element_type=f32) + jnp.dot(
            table, x_ref[t1, 1], preferred_element_type=f32
        )
        for s in range(slots):
            own, other = slice(s * 128, (s + 1) * 128), slice(n + s * 128, n + (s + 1) * 128)
            for r in range(0, QUART, 32):
                one, two = slice(r, r + 32), slice(QUART + r, QUART + r + 32)
                le = y_ref[at, one, own] + times_i(y_ref[at, two, own])
                gr = y_ref[at, one, other] + times_i(y_ref[at, two, other])
                m1, m2 = le * gr, le * pltpu.roll(gr, 64, 1)
                p_ref[at, one, own] = (
                    jnp.where(left, m1, m2) + pltpu.roll(jnp.where(left, -m2, m1), 64, 1)
                ).astype(bf16)
        z_ref[t1] = jnp.dot(b_ref[t1], p_ref[at], preferred_element_type=f32)

    ca, cb, cc = rot_ref[0], rot_ref[1], rot_ref[2]
    for s in range(slots):
        cols = slice(s * 128, (s + 1) * 128)
        for p in range(0, NP, 2):
            one = slice(p * NL, (p + 2) * NL)
            two = slice(QUART + p * NL, QUART + (p + 2) * NL)
            z0, z1, z2, z3 = (z_ref[t, one, cols] - times_i(z_ref[t, two, cols]) for t in range(4))
            u2 = cc * z2
            a, b = z0 + u2, z0 - u2
            plus, minus = z1 + z3, times_i(z1 - z3)
            c = ca * plus + cb * minus
            d = ca * minus - cb * plus
            for j, v in enumerate((a + c, b - d, a - c, b + d)):
                v = v.astype(bf16).reshape(2, NL, 128)
                if split:
                    outs[j][p : p + 2, s] = v
                else:
                    outs[0][p : p + 2, j, s] = v


def correlate(rot, inputs, fwd, inv, split, flops):
    slots = inputs[0].shape[-3]
    n = slots * 128
    vmem = pl.BlockSpec(memory_space=pltpu.VMEM)
    hbm = pl.BlockSpec(memory_space=pltpu.HBM)
    piece = jax.ShapeDtypeStruct((NP, slots, NL, 128), jnp.bfloat16)
    whole = jax.ShapeDtypeStruct((NP, NZ, slots, NL, 128), jnp.bfloat16)
    out = pl.pallas_call(
        functools.partial(correlate_kernel, slots, len(inputs), split),
        out_shape=[piece] * 4 if split else [whole],
        in_specs=[pl.BlockSpec(memory_space=pltpu.SMEM)] + [vmem] * len(inputs) + [hbm] * 2,
        out_specs=[vmem] * (4 if split else 1),
        scratch_shapes=[
            pltpu.VMEM((4, 2, QUART, 2 * n), jnp.bfloat16),
            pltpu.VMEM((BUF, QUART, n), jnp.bfloat16),
            pltpu.VMEM((BUF, 2 * QUART, 2 * n), jnp.float32),
            pltpu.VMEM((4, 2 * QUART, n), jnp.float32),
            pltpu.VMEM((4, 2 * QUART, QUART), jnp.bfloat16),
            pltpu.VMEM((4, 2 * QUART, QUART), jnp.bfloat16),
            pltpu.SemaphoreType.DMA((2, 4)),
        ],
        compiler_params=pltpu.CompilerParams(vmem_limit_bytes=52 << 20),
        cost_estimate=pl.CostEstimate(
            flops=flops, bytes_accessed=3 * NE * n * 2 + (2 << 20), transcendentals=0
        ),
        name="correlate",
    )(rot, *inputs, fwd, inv)
    return out if split else out[0]


def turning():
    row = lax.broadcasted_iota(jnp.int32, (256, 256), 0)
    col = lax.broadcasted_iota(jnp.int32, (256, 256), 1)
    return jnp.where((row % 16) * 16 + row // 16 == col, 1.0, 0.0).astype(jnp.bfloat16)


def prepare_kernel(cut, turn_ref, less_ref, great_ref, *refs):
    early_ref, late_refs, turn, held, sem = refs[0], refs[1:5], refs[5], refs[6], refs[7]
    slots = less_ref.shape[1]
    loads = [
        [pltpu.make_async_copy(ref.at[:, s], held.at[s, k], sem.at[s, k]) for k, ref in enumerate((less_ref, great_ref))]
        for s in range(slots)
    ]
    order = [*range(cut, slots), *range(cut)]
    for s in order:
        for load in loads[s]:
            load.start()
    turn[...] = turning()
    for s in order:
        for load in loads[s]:
            load.wait()
        for j in range(4):
            q = lax.rem(turn_ref[0] + 4 - j, 4)
            at = pl.ds(pl.multiple_of(q * NP, NP), NP)
            x = jnp.concatenate([held[s, k, :, at, :].reshape(256, 128) for k in range(2)], 1)
            x = jnp.dot(turn[...], x, preferred_element_type=jnp.float32).astype(jnp.bfloat16)
            for k in range(2):
                v = x[:, k * 128 : (k + 1) * 128].reshape(NP, NL, 128)
                if s < cut:
                    early_ref[:, j, k, s] = v
                else:
                    late_refs[j][:, k, s - cut] = v


def prepare(turn, less, great, cut):
    el, slots, bi, wide = less.shape
    vmem = pl.BlockSpec(memory_space=pltpu.VMEM)
    hbm = pl.BlockSpec(memory_space=pltpu.HBM)
    piece = jax.ShapeDtypeStruct((NP, 2, slots - cut, el, wide), jnp.bfloat16)
    early, *late = pl.pallas_call(
        functools.partial(prepare_kernel, cut),
        out_shape=[jax.ShapeDtypeStruct((NP, NZ, 2, cut, el, wide), jnp.bfloat16)] + [piece] * 4,
        in_specs=[pl.BlockSpec(memory_space=pltpu.SMEM), hbm, hbm],
        out_specs=[vmem] * 5,
        scratch_shapes=[
            pltpu.VMEM((256, 256), jnp.bfloat16),
            pltpu.VMEM((slots, 2, el, bi, wide), jnp.bfloat16),
            pltpu.SemaphoreType.DMA((slots, 2)),
        ],
        compiler_params=pltpu.CompilerParams(vmem_limit_bytes=60 << 20),
        cost_estimate=pl.CostEstimate(flops=0, bytes_accessed=4 * el * slots * bi * wide * 2, transcendentals=0),
        name="prepare",
    )(turn, less, great)
    return early, late


def settle_kernel(slots, pieces, *refs):
    in_refs, out_ref, turn = refs[:pieces], refs[-2], refs[-1]
    turn[...] = turning()
    for k, j in enumerate(ORDER[::-1]):
        x = [(in_refs[k][:, s] if pieces == 4 else in_refs[0][:, j, s]).reshape(256, 128) for s in range(slots)]
        x = jnp.dot(turn[...], jnp.concatenate(x, 1), preferred_element_type=jnp.float32).astype(jnp.bfloat16)
        for s in range(slots):
            out_ref[:, s, j * NP : (j + 1) * NP] = x[:, s * 128 : (s + 1) * 128].reshape(NL, NP, 128)


def settle(inputs, flops):
    slots = inputs[0].shape[-3]
    vmem = pl.BlockSpec(memory_space=pltpu.VMEM)
    return pl.pallas_call(
        functools.partial(settle_kernel, slots, len(inputs)),
        out_shape=jax.ShapeDtypeStruct((NL, slots, 64, 128), jnp.bfloat16),
        in_specs=[vmem] * len(inputs),
        out_specs=vmem,
        scratch_shapes=[pltpu.VMEM((256, 256), jnp.bfloat16)],
        cost_estimate=pl.CostEstimate(flops=flops, bytes_accessed=NL * slots * 64 * 128 * 4, transcendentals=0),
        compiler_params=pltpu.CompilerParams(vmem_limit_bytes=12 << 20),
        name="settle",
    )(*(inputs[j] for j in ORDER[::-1]) if len(inputs) == 4 else inputs)


def gather_kernel(*refs):
    for k, j in enumerate(ORDER):
        refs[4][:, j] = refs[k][...]


def gather(pieces, flops):
    shape = pieces[0].shape
    vmem = pl.BlockSpec(memory_space=pltpu.VMEM)
    return pl.pallas_call(
        gather_kernel,
        out_shape=jax.ShapeDtypeStruct((shape[0], 4, *shape[1:]), jnp.bfloat16),
        in_specs=[vmem] * 4,
        out_specs=vmem,
        cost_estimate=pl.CostEstimate(flops=flops, bytes_accessed=8 * pieces[0].size * 2, transcendentals=0),
        compiler_params=pltpu.CompilerParams(vmem_limit_bytes=12 << 20),
        name="gather",
    )(*(pieces[j] for j in ORDER))


def marker(value, pieces, flops):
    hbm = pl.BlockSpec(memory_space=pl.ANY)

    def kernel(*refs):
        refs[-1][...] = refs[0][...]

    return pl.pallas_call(
        kernel,
        out_shape=jax.ShapeDtypeStruct(value.shape, value.dtype),
        in_specs=[pl.BlockSpec(memory_space=pltpu.VMEM)] + [hbm] * len(pieces),
        out_specs=pl.BlockSpec(memory_space=pltpu.VMEM),
        cost_estimate=pl.CostEstimate(flops=flops, bytes_accessed=4096, transcendentals=0),
        compiler_params=pltpu.CompilerParams(vmem_limit_bytes=1 << 20),
        name="marker",
    )(value, *pieces)


def screen_kernel(row_ref, pattern_ref, w_ref, *refs):
    pairs, out_ref = (refs[0:2], refs[2:4], refs[4:6]), refs[6]
    slots = out_ref.shape[1]
    rows = pattern_ref.shape[0]
    row = row_ref[0]
    found = {}
    for d, step in ((0, -1), (2, 1)):
        k = row + step
        inside = jnp.logical_and(k >= 0, k < rows)
        k = jnp.clip(k, 0, rows - 1)
        for s in range(slots):
            want = pattern_ref[row, s]
            at, hit = jnp.int32(0), jnp.int32(0)
            for t in range(slots):
                same = jnp.logical_and(inside, pattern_ref[k, t] == want)
                at = jnp.where(same, t, at)
                hit = jnp.where(same, 1, hit)
            found[d, s] = at, hit
    w = w_ref[...]
    for l in range(out_ref.shape[0]):
        cols = []
        for s in range(slots):
            blocks = []
            for d, (low, high) in enumerate(pairs):
                cut = low.shape[1]
                if d == 1:
                    blocks.append(low[l, s] if s < cut else high[l, s - cut])
                else:
                    at, hit = found[d, s]
                    one = low[l, jnp.minimum(at, cut - 1)]
                    two = high[l, jnp.maximum(at - cut, 0)]
                    got = jnp.where(at < cut, one, two)
                    blocks.append(jnp.where(hit > 0, got, jnp.zeros_like(got)))
            cols.append(jnp.concatenate(blocks, 0))
        res = jnp.dot(w, jnp.concatenate(cols, 1), preferred_element_type=jnp.float32)
        for s in range(slots):
            out_ref[l, s] = res[:, s * 128 : (s + 1) * 128].astype(jnp.bfloat16)


def screen(row, pattern, weights, up, own, down):
    step = 4
    smem = pl.BlockSpec(memory_space=pltpu.SMEM)
    arrays = [*up, *own, *down]
    blocks = [pl.BlockSpec((step, *a.shape[1:]), lambda i: (i, 0, 0, 0)) for a in arrays]
    el, _, bi, wide = own[0].shape
    slots = own[0].shape[1] + own[1].shape[1]
    return pl.pallas_call(
        screen_kernel,
        grid=(el // step,),
        out_shape=jax.ShapeDtypeStruct((el, slots, bi, wide), jnp.bfloat16),
        in_specs=[smem, smem, pl.BlockSpec(weights.shape, lambda i: (0, 0)), *blocks],
        out_specs=pl.BlockSpec((step, slots, bi, wide), lambda i: (i, 0, 0, 0)),
        cost_estimate=pl.CostEstimate(
            flops=2 * el * slots * bi * 3 * bi * wide, bytes_accessed=8 * el * slots * bi * wide, transcendentals=0
        ),
        compiler_params=pltpu.CompilerParams(vmem_limit_bytes=12 << 20),
        name="screen",
    )(row, pattern, weights, *arrays)


def shards(g_less, g_greater, coulomb, pattern):
    el, rows, slots, bi, wide = g_less.shape
    iz, s_row = lax.axis_index("z"), lax.axis_index("s")
    z_lo = s_row // 2
    turn = iz + z_lo + 1
    fwd, inv = (jnp.asarray(t) for t in tables())

    def piece_of(arr, j, axis, size):
        q = (turn + 4 - j) % 4
        return lax.dynamic_slice_in_dim(arr, q * size, size, axis)

    c = turn % 4
    rot = jnp.stack([
        jnp.where(c == 0, 1.0, jnp.where(c == 2, -1.0, 0.0)),
        jnp.where(c == 1, 1.0, jnp.where(c == 3, -1.0, 0.0)),
        jnp.where(c % 2 == 0, 1.0, -1.0),
    ]).astype(jnp.float32)
    near = (s_row + jnp.arange(3) - 1 + 4) % 4 // 2
    order = (iz + near[:, None] + 2 + jnp.arange(4)[None, :]) % 4
    pick = (order[:, :, None] == jnp.arange(4)[None, None, :]).astype(jnp.bfloat16)
    weights = jnp.einsum(
        "djq,adqp->adjp", pick, coulomb.reshape(bi, 3, NZ, NP), preferred_element_type=jnp.float32
    ).astype(jnp.bfloat16).reshape(bi, 3 * bi)

    cut = CUT
    both = (g_less.reshape(el, slots, bi, wide), g_greater.reshape(el, slots, bi, wide))
    early, late = prepare((turn % 4).reshape(1), *both, cut)
    late = gather([hop(late[j], STEPS[j]) for j in range(4)], HEAVY)
    early = lax.all_to_all(early, PLANE, split_axis=0, concat_axis=0, tiled=True)
    early = after(early, late)
    early = [hop(early[:, j], STEPS[j]) for j in range(4)]
    late = lax.all_to_all(late, PLANE, split_axis=0, concat_axis=0, tiled=True)

    late, rot = lax.optimization_barrier([late, marker(rot, early[1:3], HEAVY)])
    hi = correlate(rot, [late], fwd, inv, False, 0)
    early[0] = after(early[0], hi)
    lo = correlate(rot, early, fwd, inv, True, HEAVY)

    hi = lax.all_to_all(hi, PLANE, split_axis=0, concat_axis=0, tiled=True)
    lo = gather([hop(p, STEPS[j]) for j, p in enumerate(lo)], 0)
    hi = settle([hop(hi[:, j], STEPS[j]) for j in range(4)], HEAVY)
    lo = lax.all_to_all(lo, PLANE, split_axis=0, concat_axis=0, tiled=True)
    lo = settle([after(lo, hi)], 0)

    def halo(cells):
        up = lax.ppermute(cells, "s", [(0, 1), (1, 2), (2, 3)])
        down = lax.ppermute(cells, "s", [(1, 0), (2, 1), (3, 2)])
        return up, down

    up_hi, down_hi = halo(hi)
    lo = lax.optimization_barrier([lo, up_hi, down_hi])[0]
    up_lo, down_lo = halo(lo)
    return screen(s_row.reshape(1), pattern, weights, (up_lo, up_hi), (lo, hi), (down_lo, down_hi))[:, None]


def solution(mesh):
    fine = Mesh(mesh.devices.reshape(4, 4, 4, 4), ALL)
    energy = ("z", "y", "x")
    return jax.shard_map(
        shards,
        mesh=fine,
        in_specs=(P(energy, "s"), P(energy, "s"), P("s"), P()),
        out_specs=P(energy, "s"),
        check_vma=False,
    )
```

```python
import functools
import math

import jax
import jax.numpy as jnp
import ml_dtypes
import numpy as np
from jax import lax
from jax.experimental import pallas as pl
from jax.experimental.pallas import tpu as pltpu
from jax.sharding import Mesh, PartitionSpec as P

NE = 1024
QUART = NE // 4
NZ = 4
NP = 16
NL = 16
ALL = ("z", "y", "x", "s")
PLANE = ("y", "x")
CUT = 3
ORDER = (0, 3, 1, 2)
BUF = 2
HEAVY = 100 * 10**9
STEPS = (3, 1, -1, -3)


def tables():
    e = np.arange(QUART)
    out = []
    for first in range(4):
        t = 4 * np.arange(QUART) + first
        angle = 2.0 * math.pi * ((e[:, None] * t[None, :]) % NE) / NE
        scale = 1.0 / math.sqrt(NE)
        real = (np.cos(angle) * scale).astype(np.float32).astype(ml_dtypes.bfloat16)
        imag = (-np.sin(angle) * scale).astype(np.float32).astype(ml_dtypes.bfloat16)
        out.append((real, imag))
    forward = np.stack([np.concatenate([r.T, i.T]) for r, i in out])
    inverse = np.stack([np.concatenate([r, i]) for r, i in out])
    return forward, inverse


def after(value, other):
    return lax.optimization_barrier([value, other])[0]


def hop(piece, step):
    perm = []
    for z in range(4):
        for yx in range(16):
            for s in range(4):
                to = (2 * z + s // 2 + step) % 8
                perm.append(((z * 16 + yx) * 4 + s, ((to // 2) * 16 + yx) * 4 + (to % 2) * 2 + s % 2))
    return lax.ppermute(piece, ALL, perm)


def times_i(v):
    lane = lax.broadcasted_iota(jnp.int32, v.shape, 1)
    return jnp.where(lane < 64, -1.0, 1.0) * pltpu.roll(v, 64, 1)


def correlate_kernel(slots, pieces, split, rot_ref, *refs):
    in_refs, fwd_ref, inv_ref = refs[:pieces], refs[pieces], refs[pieces + 1]
    n_out = 4 if split else 1
    outs = refs[pieces + 2 : pieces + 2 + n_out]
    x_ref, p_ref, y_ref, z_ref, f_ref, b_ref, sem = refs[pieces + 2 + n_out :]
    loads = [
        [pltpu.make_async_copy(ref.at[t1], held.at[t1], sem.at[k, t1]) for t1 in range(4)]
        for k, (ref, held) in enumerate(((fwd_ref, f_ref), (inv_ref, b_ref)))
    ]
    for t1 in range(4):
        for k in range(2):
            loads[k][t1].start()
    f32, bf16 = jnp.float32, jnp.bfloat16
    left = lax.broadcasted_iota(jnp.int32, (32, 128), 1) < 64

    def fetch(j, which, s, p):
        ref = in_refs[j][p : p + 2, which, s] if pieces == 4 else in_refs[0][p : p + 2, j, which, s]
        return ref.reshape(2 * NL, 128).astype(f32)

    for s in range(slots):
        for which in range(2):
            cols = slice((which * slots + s) * 128, (which * slots + s + 1) * 128)
            for p in range(0, NP, 2):
                rows = slice(p * NL, (p + 2) * NL)
                x0, x1, x2, x3 = (fetch(j, which, s, p) for j in range(4))
                a, b, c, d = x0 + x2, x0 - x2, x1 + x3, times_i(x1 - x3)
                for t1, v in enumerate((a + c, b - d, a - c, b + d)):
                    hi = v.astype(bf16)
                    x_ref[t1, 0, rows, cols] = hi
                    x_ref[t1, 1, rows, cols] = (v - hi.astype(f32)).astype(bf16)

    n = slots * 128
    for t1 in range(4):
        loads[0][t1].wait()
        loads[1][t1].wait()
        table, at = f_ref[t1], t1 % BUF
        y_ref[at] = jnp.dot(table, x_ref[t1, 0], preferred_element_type=f32) + jnp.dot(
            table, x_ref[t1, 1], preferred_element_type=f32
        )
        for s in range(slots):
            own, other = slice(s * 128, (s + 1) * 128), slice(n + s * 128, n + (s + 1) * 128)
            for r in range(0, QUART, 32):
                one, two = slice(r, r + 32), slice(QUART + r, QUART + r + 32)
                le = y_ref[at, one, own] + times_i(y_ref[at, two, own])
                gr = y_ref[at, one, other] + times_i(y_ref[at, two, other])
                m1, m2 = le * gr, le * pltpu.roll(gr, 64, 1)
                p_ref[at, one, own] = (
                    jnp.where(left, m1, m2) + pltpu.roll(jnp.where(left, -m2, m1), 64, 1)
                ).astype(bf16)
        z_ref[t1] = jnp.dot(b_ref[t1], p_ref[at], preferred_element_type=f32)

    ca, cb, cc = rot_ref[0], rot_ref[1], rot_ref[2]
    for s in range(slots):
        cols = slice(s * 128, (s + 1) * 128)
        for p in range(0, NP, 2):
            one = slice(p * NL, (p + 2) * NL)
            two = slice(QUART + p * NL, QUART + (p + 2) * NL)
            z0, z1, z2, z3 = (z_ref[t, one, cols] - times_i(z_ref[t, two, cols]) for t in range(4))
            u2 = cc * z2
            a, b = z0 + u2, z0 - u2
            plus, minus = z1 + z3, times_i(z1 - z3)
            c = ca * plus + cb * minus
            d = ca * minus - cb * plus
            for j, v in enumerate((a + c, b - d, a - c, b + d)):
                v = v.astype(bf16).reshape(2, NL, 128)
                if split:
                    outs[j][p : p + 2, s] = v
                else:
                    outs[0][p : p + 2, j, s] = v


def correlate(rot, inputs, fwd, inv, split, flops):
    slots = inputs[0].shape[-3]
    n = slots * 128
    vmem = pl.BlockSpec(memory_space=pltpu.VMEM)
    hbm = pl.BlockSpec(memory_space=pltpu.HBM)
    piece = jax.ShapeDtypeStruct((NP, slots, NL, 128), jnp.bfloat16)
    whole = jax.ShapeDtypeStruct((NP, NZ, slots, NL, 128), jnp.bfloat16)
    out = pl.pallas_call(
        functools.partial(correlate_kernel, slots, len(inputs), split),
        out_shape=[piece] * 4 if split else [whole],
        in_specs=[pl.BlockSpec(memory_space=pltpu.SMEM)] + [vmem] * len(inputs) + [hbm] * 2,
        out_specs=[vmem] * (4 if split else 1),
        scratch_shapes=[
            pltpu.VMEM((4, 2, QUART, 2 * n), jnp.bfloat16),
            pltpu.VMEM((BUF, QUART, n), jnp.bfloat16),
            pltpu.VMEM((BUF, 2 * QUART, 2 * n), jnp.float32),
            pltpu.VMEM((4, 2 * QUART, n), jnp.float32),
            pltpu.VMEM((4, 2 * QUART, QUART), jnp.bfloat16),
            pltpu.VMEM((4, 2 * QUART, QUART), jnp.bfloat16),
            pltpu.SemaphoreType.DMA((2, 4)),
        ],
        compiler_params=pltpu.CompilerParams(vmem_limit_bytes=52 << 20),
        cost_estimate=pl.CostEstimate(
            flops=flops, bytes_accessed=3 * NE * n * 2 + (2 << 20), transcendentals=0
        ),
        name="correlate",
    )(rot, *inputs, fwd, inv)
    return out if split else out[0]


def turning():
    row = lax.broadcasted_iota(jnp.int32, (256, 256), 0)
    col = lax.broadcasted_iota(jnp.int32, (256, 256), 1)
    return jnp.where((row % 16) * 16 + row // 16 == col, 1.0, 0.0).astype(jnp.bfloat16)


def prepare_kernel(cut, turn_ref, less_ref, great_ref, *refs):
    early_ref, late_refs, turn, held, sem = refs[0], refs[1:5], refs[5], refs[6], refs[7]
    slots = less_ref.shape[1]
    loads = [
        [pltpu.make_async_copy(ref.at[:, s], held.at[s, k], sem.at[s, k]) for k, ref in enumerate((less_ref, great_ref))]
        for s in range(slots)
    ]
    order = [*range(cut, slots), *range(cut)]
    for s in order:
        for load in loads[s]:
            load.start()
    turn[...] = turning()
    for s in order:
        for load in loads[s]:
            load.wait()
        for j in range(4):
            q = lax.rem(turn_ref[0] + 4 - j, 4)
            at = pl.ds(pl.multiple_of(q * NP, NP), NP)
            x = jnp.concatenate([held[s, k, :, at, :].reshape(256, 128) for k in range(2)], 1)
            x = jnp.dot(turn[...], x, preferred_element_type=jnp.float32).astype(jnp.bfloat16)
            for k in range(2):
                v = x[:, k * 128 : (k + 1) * 128].reshape(NP, NL, 128)
                if s < cut:
                    early_ref[:, j, k, s] = v
                else:
                    late_refs[j][:, k, s - cut] = v


def prepare(turn, less, great, cut):
    el, slots, bi, wide = less.shape
    vmem = pl.BlockSpec(memory_space=pltpu.VMEM)
    hbm = pl.BlockSpec(memory_space=pltpu.HBM)
    piece = jax.ShapeDtypeStruct((NP, 2, slots - cut, el, wide), jnp.bfloat16)
    early, *late = pl.pallas_call(
        functools.partial(prepare_kernel, cut),
        out_shape=[jax.ShapeDtypeStruct((NP, NZ, 2, cut, el, wide), jnp.bfloat16)] + [piece] * 4,
        in_specs=[pl.BlockSpec(memory_space=pltpu.SMEM), hbm, hbm],
        out_specs=[vmem] * 5,
        scratch_shapes=[
            pltpu.VMEM((256, 256), jnp.bfloat16),
            pltpu.VMEM((slots, 2, el, bi, wide), jnp.bfloat16),
            pltpu.SemaphoreType.DMA((slots, 2)),
        ],
        compiler_params=pltpu.CompilerParams(vmem_limit_bytes=60 << 20),
        cost_estimate=pl.CostEstimate(flops=0, bytes_accessed=4 * el * slots * bi * wide * 2, transcendentals=0),
        name="prepare",
    )(turn, less, great)
    return early, late


def settle_kernel(slots, pieces, *refs):
    in_refs, out_ref, turn = refs[:pieces], refs[-2], refs[-1]
    turn[...] = turning()
    for k, j in enumerate(ORDER[::-1]):
        x = [(in_refs[k][:, s] if pieces == 4 else in_refs[0][:, j, s]).reshape(256, 128) for s in range(slots)]
        x = jnp.dot(turn[...], jnp.concatenate(x, 1), preferred_element_type=jnp.float32).astype(jnp.bfloat16)
        for s in range(slots):
            out_ref[:, s, j * NP : (j + 1) * NP] = x[:, s * 128 : (s + 1) * 128].reshape(NL, NP, 128)


def settle(inputs, flops):
    slots = inputs[0].shape[-3]
    vmem = pl.BlockSpec(memory_space=pltpu.VMEM)
    return pl.pallas_call(
        functools.partial(settle_kernel, slots, len(inputs)),
        out_shape=jax.ShapeDtypeStruct((NL, slots, 64, 128), jnp.bfloat16),
        in_specs=[vmem] * len(inputs),
        out_specs=vmem,
        scratch_shapes=[pltpu.VMEM((256, 256), jnp.bfloat16)],
        cost_estimate=pl.CostEstimate(flops=flops, bytes_accessed=NL * slots * 64 * 128 * 4, transcendentals=0),
        compiler_params=pltpu.CompilerParams(vmem_limit_bytes=12 << 20),
        name="settle",
    )(*(inputs[j] for j in ORDER[::-1]) if len(inputs) == 4 else inputs)


def gather_kernel(*refs):
    for k, j in enumerate(ORDER):
        refs[4][:, j] = refs[k][...]


def gather(pieces, flops):
    shape = pieces[0].shape
    vmem = pl.BlockSpec(memory_space=pltpu.VMEM)
    return pl.pallas_call(
        gather_kernel,
        out_shape=jax.ShapeDtypeStruct((shape[0], 4, *shape[1:]), jnp.bfloat16),
        in_specs=[vmem] * 4,
        out_specs=vmem,
        cost_estimate=pl.CostEstimate(flops=flops, bytes_accessed=8 * pieces[0].size * 2, transcendentals=0),
        compiler_params=pltpu.CompilerParams(vmem_limit_bytes=12 << 20),
        name="gather",
    )(*(pieces[j] for j in ORDER))


def marker(value, pieces, flops):
    hbm = pl.BlockSpec(memory_space=pl.ANY)

    def kernel(*refs):
        refs[-1][...] = refs[0][...]

    return pl.pallas_call(
        kernel,
        out_shape=jax.ShapeDtypeStruct(value.shape, value.dtype),
        in_specs=[pl.BlockSpec(memory_space=pltpu.VMEM)] + [hbm] * len(pieces),
        out_specs=pl.BlockSpec(memory_space=pltpu.VMEM),
        cost_estimate=pl.CostEstimate(flops=flops, bytes_accessed=4096, transcendentals=0),
        compiler_params=pltpu.CompilerParams(vmem_limit_bytes=1 << 20),
        name="marker",
    )(value, *pieces)


def screen_kernel(row_ref, pattern_ref, w_ref, *refs):
    pairs, out_ref = (refs[0:2], refs[2:4], refs[4:6]), refs[6]
    slots = out_ref.shape[1]
    rows = pattern_ref.shape[0]
    row = row_ref[0]
    found = {}
    for d, step in ((0, -1), (2, 1)):
        k = row + step
        inside = jnp.logical_and(k >= 0, k < rows)
        k = jnp.clip(k, 0, rows - 1)
        for s in range(slots):
            want = pattern_ref[row, s]
            at, hit = jnp.int32(0), jnp.int32(0)
            for t in range(slots):
                same = jnp.logical_and(inside, pattern_ref[k, t] == want)
                at = jnp.where(same, t, at)
                hit = jnp.where(same, 1, hit)
            found[d, s] = at, hit
    w = w_ref[...]
    for l in range(out_ref.shape[0]):
        cols = []
        for s in range(slots):
            blocks = []
            for d, (low, high) in enumerate(pairs):
                cut = low.shape[1]
                if d == 1:
                    blocks.append(low[l, s] if s < cut else high[l, s - cut])
                else:
                    at, hit = found[d, s]
                    one = low[l, jnp.minimum(at, cut - 1)]
                    two = high[l, jnp.maximum(at - cut, 0)]
                    got = jnp.where(at < cut, one, two)
                    blocks.append(jnp.where(hit > 0, got, jnp.zeros_like(got)))
            cols.append(jnp.concatenate(blocks, 0))
        res = jnp.dot(w, jnp.concatenate(cols, 1), preferred_element_type=jnp.float32)
        for s in range(slots):
            out_ref[l, s] = res[:, s * 128 : (s + 1) * 128].astype(jnp.bfloat16)


def screen(row, pattern, weights, up, own, down):
    step = 4
    smem = pl.BlockSpec(memory_space=pltpu.SMEM)
    arrays = [*up, *own, *down]
    blocks = [pl.BlockSpec((step, *a.shape[1:]), lambda i: (i, 0, 0, 0)) for a in arrays]
    el, _, bi, wide = own[0].shape
    slots = own[0].shape[1] + own[1].shape[1]
    return pl.pallas_call(
        screen_kernel,
        grid=(el // step,),
        out_shape=jax.ShapeDtypeStruct((el, slots, bi, wide), jnp.bfloat16),
        in_specs=[smem, smem, pl.BlockSpec(weights.shape, lambda i: (0, 0)), *blocks],
        out_specs=pl.BlockSpec((step, slots, bi, wide), lambda i: (i, 0, 0, 0)),
        cost_estimate=pl.CostEstimate(
            flops=2 * el * slots * bi * 3 * bi * wide, bytes_accessed=8 * el * slots * bi * wide, transcendentals=0
        ),
        compiler_params=pltpu.CompilerParams(vmem_limit_bytes=12 << 20),
        name="screen",
    )(row, pattern, weights, *arrays)


def shards(g_less, g_greater, coulomb, pattern):
    el, rows, slots, bi, wide = g_less.shape
    iz, s_row = lax.axis_index("z"), lax.axis_index("s")
    z_lo = s_row // 2
    turn = iz + z_lo + 1
    fwd, inv = (jnp.asarray(t) for t in tables())

    def piece_of(arr, j, axis, size):
        q = (turn + 4 - j) % 4
        return lax.dynamic_slice_in_dim(arr, q * size, size, axis)

    c = turn % 4
    rot = jnp.stack([
        jnp.where(c == 0, 1.0, jnp.where(c == 2, -1.0, 0.0)),
        jnp.where(c == 1, 1.0, jnp.where(c == 3, -1.0, 0.0)),
        jnp.where(c % 2 == 0, 1.0, -1.0),
    ]).astype(jnp.float32)
    near = (s_row + jnp.arange(3) - 1 + 4) % 4 // 2
    order = (iz + near[:, None] + 2 + jnp.arange(4)[None, :]) % 4
    pick = (order[:, :, None] == jnp.arange(4)[None, None, :]).astype(jnp.bfloat16)
    weights = jnp.einsum(
        "djq,adqp->adjp", pick, coulomb.reshape(bi, 3, NZ, NP), preferred_element_type=jnp.float32
    ).astype(jnp.bfloat16).reshape(bi, 3 * bi)

    cut = CUT
    both = (g_less.reshape(el, slots, bi, wide), g_greater.reshape(el, slots, bi, wide))
    early, late = prepare((turn % 4).reshape(1), *both, cut)
    late = [hop(late[j], STEPS[j]) for j in range(4)]
    late[1], rot = lax.optimization_barrier([late[1], marker(rot, [late[0], late[3]], HEAVY)])
    late = gather(late, 0)
    early = lax.all_to_all(early, PLANE, split_axis=0, concat_axis=0, tiled=True)
    early = after(early, late)
    early = [hop(early[:, j], STEPS[j]) for j in range(4)]
    late = lax.all_to_all(late, PLANE, split_axis=0, concat_axis=0, tiled=True)

    late, rot = lax.optimization_barrier([late, marker(rot, early[1:3], HEAVY)])
    hi = correlate(rot, [late], fwd, inv, False, 0)
    early[0] = after(early[0], hi)
    lo = correlate(rot, early, fwd, inv, True, HEAVY)

    hi = lax.all_to_all(hi, PLANE, split_axis=0, concat_axis=0, tiled=True)
    lo = gather([hop(p, STEPS[j]) for j, p in enumerate(lo)], 0)
    hi = settle([hop(hi[:, j], STEPS[j]) for j in range(4)], HEAVY)
    lo = lax.all_to_all(lo, PLANE, split_axis=0, concat_axis=0, tiled=True)
    lo = settle([after(lo, hi)], 0)

    def halo(cells):
        up = lax.ppermute(cells, "s", [(0, 1), (1, 2), (2, 3)])
        down = lax.ppermute(cells, "s", [(1, 0), (2, 1), (3, 2)])
        return up, down

    up_hi, down_hi = halo(hi)
    lo = lax.optimization_barrier([lo, up_hi, down_hi])[0]
    up_lo, down_lo = halo(lo)
    return screen(s_row.reshape(1), pattern, weights, (up_lo, up_hi), (lo, hi), (down_lo, down_hi))[:, None]


def solution(mesh):
    fine = Mesh(mesh.devices.reshape(4, 4, 4, 4), ALL)
    energy = ("z", "y", "x")
    return jax.shard_map(
        shards,
        mesh=fine,
        in_specs=(P(energy, "s"), P(energy, "s"), P("s"), P()),
        out_specs=P(energy, "s"),
        check_vma=False,
    )
```

```python
import functools
import math

import jax
import jax.numpy as jnp
import ml_dtypes
import numpy as np
from jax import lax
from jax.experimental import pallas as pl
from jax.experimental.pallas import tpu as pltpu
from jax.sharding import Mesh, PartitionSpec as P

NE = 1024
QUART = NE // 4
NZ = 4
NP = 16
NL = 16
ALL = ("z", "y", "x", "s")
PLANE = ("y", "x")
CUT = 3
ORDER = (0, 3, 1, 2)
BUF = 2
ROOM_HI, ROOM_LO = 52, 52
HEAVY = 100 * 10**9
STEPS = (3, 1, -1, -3)


def tables():
    e = np.arange(QUART)
    out = []
    for first in range(4):
        t = 4 * np.arange(QUART) + first
        angle = 2.0 * math.pi * ((e[:, None] * t[None, :]) % NE) / NE
        scale = 1.0 / math.sqrt(NE)
        real = (np.cos(angle) * scale).astype(np.float32).astype(ml_dtypes.bfloat16)
        imag = (-np.sin(angle) * scale).astype(np.float32).astype(ml_dtypes.bfloat16)
        out.append((real, imag))
    forward = np.stack([np.concatenate([r.T, i.T]) for r, i in out])
    inverse = np.stack([np.concatenate([r, i]) for r, i in out])
    return forward, inverse


def after(value, other):
    return lax.optimization_barrier([value, other])[0]


def hop(piece, step):
    perm = []
    for z in range(4):
        for yx in range(16):
            for s in range(4):
                to = (2 * z + s // 2 + step) % 8
                perm.append(((z * 16 + yx) * 4 + s, ((to // 2) * 16 + yx) * 4 + (to % 2) * 2 + s % 2))
    return lax.ppermute(piece, ALL, perm)


def times_i(v):
    lane = lax.broadcasted_iota(jnp.int32, v.shape, 1)
    return jnp.where(lane < 64, -1.0, 1.0) * pltpu.roll(v, 64, 1)


def correlate_kernel(slots, pieces, split, rot_ref, *refs):
    in_refs, fwd_ref, inv_ref = refs[:pieces], refs[pieces], refs[pieces + 1]
    n_out = 4 if split else 1
    outs = refs[pieces + 2 : pieces + 2 + n_out]
    x_ref, p_ref, y_ref, z_ref, f_ref, b_ref, sem = refs[pieces + 2 + n_out :]
    loads = [
        [pltpu.make_async_copy(ref.at[t1], held.at[t1], sem.at[k, t1]) for t1 in range(4)]
        for k, (ref, held) in enumerate(((fwd_ref, f_ref), (inv_ref, b_ref)))
    ]
    for t1 in range(4):
        for k in range(2):
            loads[k][t1].start()
    f32, bf16 = jnp.float32, jnp.bfloat16
    left = lax.broadcasted_iota(jnp.int32, (32, 128), 1) < 64

    def fetch(j, which, s, p):
        ref = in_refs[j][p : p + 2, which, s] if pieces == 4 else in_refs[0][p : p + 2, j, which, s]
        return ref.reshape(2 * NL, 128).astype(f32)

    for s in range(slots):
        for which in range(2):
            cols = slice((which * slots + s) * 128, (which * slots + s + 1) * 128)
            for p in range(0, NP, 2):
                rows = slice(p * NL, (p + 2) * NL)
                x0, x1, x2, x3 = (fetch(j, which, s, p) for j in range(4))
                a, b, c, d = x0 + x2, x0 - x2, x1 + x3, times_i(x1 - x3)
                for t1, v in enumerate((a + c, b - d, a - c, b + d)):
                    hi = v.astype(bf16)
                    x_ref[t1, 0, rows, cols] = hi
                    x_ref[t1, 1, rows, cols] = (v - hi.astype(f32)).astype(bf16)

    n = slots * 128
    for t1 in range(4):
        loads[0][t1].wait()
        loads[1][t1].wait()
        table, at = f_ref[t1], t1 % BUF
        y_ref[at] = jnp.dot(table, x_ref[t1, 0], preferred_element_type=f32) + jnp.dot(
            table, x_ref[t1, 1], preferred_element_type=f32
        )
        for s in range(slots):
            own, other = slice(s * 128, (s + 1) * 128), slice(n + s * 128, n + (s + 1) * 128)
            for r in range(0, QUART, 32):
                one, two = slice(r, r + 32), slice(QUART + r, QUART + r + 32)
                le = y_ref[at, one, own] + times_i(y_ref[at, two, own])
                gr = y_ref[at, one, other] + times_i(y_ref[at, two, other])
                m1, m2 = le * gr, le * pltpu.roll(gr, 64, 1)
                p_ref[at, one, own] = (
                    jnp.where(left, m1, m2) + pltpu.roll(jnp.where(left, -m2, m1), 64, 1)
                ).astype(bf16)
        z_ref[t1] = jnp.dot(b_ref[t1], p_ref[at], preferred_element_type=f32)

    ca, cb, cc = rot_ref[0], rot_ref[1], rot_ref[2]
    for s in range(slots):
        cols = slice(s * 128, (s + 1) * 128)
        for p in range(0, NP, 2):
            one = slice(p * NL, (p + 2) * NL)
            two = slice(QUART + p * NL, QUART + (p + 2) * NL)
            z0, z1, z2, z3 = (z_ref[t, one, cols] - times_i(z_ref[t, two, cols]) for t in range(4))
            u2 = cc * z2
            a, b = z0 + u2, z0 - u2
            plus, minus = z1 + z3, times_i(z1 - z3)
            c = ca * plus + cb * minus
            d = ca * minus - cb * plus
            for j, v in enumerate((a + c, b - d, a - c, b + d)):
                v = v.astype(bf16).reshape(2, NL, 128)
                if split:
                    outs[j][p : p + 2, s] = v
                else:
                    outs[0][p : p + 2, j, s] = v


def correlate(rot, inputs, fwd, inv, split, flops, room):
    slots = inputs[0].shape[-3]
    n = slots * 128
    vmem = pl.BlockSpec(memory_space=pltpu.VMEM)
    hbm = pl.BlockSpec(memory_space=pltpu.HBM)
    piece = jax.ShapeDtypeStruct((NP, slots, NL, 128), jnp.bfloat16)
    whole = jax.ShapeDtypeStruct((NP, NZ, slots, NL, 128), jnp.bfloat16)
    out = pl.pallas_call(
        functools.partial(correlate_kernel, slots, len(inputs), split),
        out_shape=[piece] * 4 if split else [whole],
        in_specs=[pl.BlockSpec(memory_space=pltpu.SMEM)] + [vmem] * len(inputs) + [hbm] * 2,
        out_specs=[vmem] * (4 if split else 1),
        scratch_shapes=[
            pltpu.VMEM((4, 2, QUART, 2 * n), jnp.bfloat16),
            pltpu.VMEM((BUF, QUART, n), jnp.bfloat16),
            pltpu.VMEM((BUF, 2 * QUART, 2 * n), jnp.float32),
            pltpu.VMEM((4, 2 * QUART, n), jnp.float32),
            pltpu.VMEM((4, 2 * QUART, QUART), jnp.bfloat16),
            pltpu.VMEM((4, 2 * QUART, QUART), jnp.bfloat16),
            pltpu.SemaphoreType.DMA((2, 4)),
        ],
        compiler_params=pltpu.CompilerParams(vmem_limit_bytes=room << 20),
        cost_estimate=pl.CostEstimate(
            flops=flops, bytes_accessed=3 * NE * n * 2 + (2 << 20), transcendentals=0
        ),
        name="correlate",
    )(rot, *inputs, fwd, inv)
    return out if split else out[0]


def turning():
    row = lax.broadcasted_iota(jnp.int32, (256, 256), 0)
    col = lax.broadcasted_iota(jnp.int32, (256, 256), 1)
    return jnp.where((row % 16) * 16 + row // 16 == col, 1.0, 0.0).astype(jnp.bfloat16)


def place_of(pattern_ref, row, slot):
    def plain(t):
        offset = pattern_ref[row, t] - row
        return jnp.logical_and(offset != 0, offset != 6)

    rank = jnp.int32(0)
    for t in range(slot):
        rank = rank + jnp.where(plain(t), 1, 0)
    other = jnp.where(rank == 0, 1, rank + 2)
    return jnp.where(plain(slot), other, jnp.where(pattern_ref[row, slot] == row, 0, 2))


def prepare_kernel(cut, turn_ref, row_ref, pattern_ref, less_ref, great_ref, *refs):
    early_ref, late_refs, turn, held, sem = refs[0], refs[1:5], refs[5], refs[6], refs[7]
    slots = less_ref.shape[1]
    places = [place_of(pattern_ref, row_ref[0], t) for t in range(slots)]
    source = []
    for s in range(slots):
        at = jnp.int32(0)
        for t in range(slots):
            at = jnp.where(places[t] == s, t, at)
        source.append(at)
    loads = [
        [pltpu.make_async_copy(ref.at[:, source[s]], held.at[s, k], sem.at[s, k]) for k, ref in enumerate((less_ref, great_ref))]
        for s in range(slots)
    ]
    order = [*range(cut, slots), *range(cut)]
    for s in order:
        for load in loads[s]:
            load.start()
    turn[...] = turning()
    for s in order:
        for load in loads[s]:
            load.wait()
        for j in range(4):
            q = lax.rem(turn_ref[0] + 4 - j, 4)
            at = pl.ds(pl.multiple_of(q * NP, NP), NP)
            x = jnp.concatenate([held[s, k, :, at, :].reshape(256, 128) for k in range(2)], 1)
            x = jnp.dot(turn[...], x, preferred_element_type=jnp.float32).astype(jnp.bfloat16)
            for k in range(2):
                v = x[:, k * 128 : (k + 1) * 128].reshape(NP, NL, 128)
                if s < cut:
                    early_ref[:, j, k, s] = v
                else:
                    late_refs[j][:, k, s - cut] = v


def prepare(turn, row, pattern, less, great, cut):
    el, slots, bi, wide = less.shape
    vmem = pl.BlockSpec(memory_space=pltpu.VMEM)
    hbm = pl.BlockSpec(memory_space=pltpu.HBM)
    piece = jax.ShapeDtypeStruct((NP, 2, slots - cut, el, wide), jnp.bfloat16)
    early, *late = pl.pallas_call(
        functools.partial(prepare_kernel, cut),
        out_shape=[jax.ShapeDtypeStruct((NP, NZ, 2, cut, el, wide), jnp.bfloat16)] + [piece] * 4,
        in_specs=[pl.BlockSpec(memory_space=pltpu.SMEM)] * 3 + [hbm, hbm],
        out_specs=[vmem] * 5,
        scratch_shapes=[
            pltpu.VMEM((256, 256), jnp.bfloat16),
            pltpu.VMEM((slots, 2, el, bi, wide), jnp.bfloat16),
            pltpu.SemaphoreType.DMA((slots, 2)),
        ],
        compiler_params=pltpu.CompilerParams(vmem_limit_bytes=60 << 20),
        cost_estimate=pl.CostEstimate(flops=0, bytes_accessed=4 * el * slots * bi * wide * 2, transcendentals=0),
        name="prepare",
    )(turn, row, pattern, less, great)
    return early, late


def settle_kernel(slots, pieces, *refs):
    in_refs, out_refs, turn = refs[:pieces], refs[pieces:-1], refs[-1]
    turn[...] = turning()
    for k, j in enumerate(ORDER[::-1]):
        x = [(in_refs[k][:, s] if pieces == 4 else in_refs[0][:, j, s]).reshape(256, 128) for s in range(slots)]
        x = jnp.dot(turn[...], jnp.concatenate(x, 1), preferred_element_type=jnp.float32).astype(jnp.bfloat16)
        for s in range(slots):
            v = x[:, s * 128 : (s + 1) * 128].reshape(NL, NP, 128)
            for out_ref, first in zip(out_refs, (0, 1, 0)):
                if 0 <= s - first < out_ref.shape[1]:
                    out_ref[:, s - first, j * NP : (j + 1) * NP] = v


def settle(inputs, parts, flops):
    slots = inputs[0].shape[-3]
    vmem = pl.BlockSpec(memory_space=pltpu.VMEM)
    counts = [slots, slots - 1, slots - 1] if parts else [slots]
    return pl.pallas_call(
        functools.partial(settle_kernel, slots, len(inputs)),
        out_shape=[jax.ShapeDtypeStruct((NL, n, 64, 128), jnp.bfloat16) for n in counts],
        in_specs=[vmem] * len(inputs),
        out_specs=[vmem] * len(counts),
        scratch_shapes=[pltpu.VMEM((256, 256), jnp.bfloat16)],
        cost_estimate=pl.CostEstimate(flops=flops, bytes_accessed=NL * slots * 64 * 128 * 4, transcendentals=0),
        compiler_params=pltpu.CompilerParams(vmem_limit_bytes=12 << 20),
        name="settle",
    )(*((inputs[j] for j in ORDER[::-1]) if len(inputs) == 4 else inputs))


def gather_kernel(*refs):
    for k, j in enumerate(ORDER):
        refs[4][:, j] = refs[k][...]


def gather(pieces, flops):
    shape = pieces[0].shape
    vmem = pl.BlockSpec(memory_space=pltpu.VMEM)
    return pl.pallas_call(
        gather_kernel,
        out_shape=jax.ShapeDtypeStruct((shape[0], 4, *shape[1:]), jnp.bfloat16),
        in_specs=[vmem] * 4,
        out_specs=vmem,
        cost_estimate=pl.CostEstimate(flops=flops, bytes_accessed=8 * pieces[0].size * 2, transcendentals=0),
        compiler_params=pltpu.CompilerParams(vmem_limit_bytes=12 << 20),
        name="gather",
    )(*(pieces[j] for j in ORDER))


def marker(value, pieces, flops):
    hbm = pl.BlockSpec(memory_space=pl.ANY)

    def kernel(*refs):
        refs[-1][...] = refs[0][...]

    return pl.pallas_call(
        kernel,
        out_shape=jax.ShapeDtypeStruct(value.shape, value.dtype),
        in_specs=[pl.BlockSpec(memory_space=pltpu.VMEM)] + [hbm] * len(pieces),
        out_specs=pl.BlockSpec(memory_space=pltpu.VMEM),
        cost_estimate=pl.CostEstimate(flops=flops, bytes_accessed=4096, transcendentals=0),
        compiler_params=pltpu.CompilerParams(vmem_limit_bytes=1 << 20),
        name="marker",
    )(value, *pieces)


def screen_kernel(row_ref, pattern_ref, w_ref, *refs):
    pairs, out_ref, at_ref = (refs[0:2], refs[2:4], refs[4:6]), refs[6], refs[7]
    slots = out_ref.shape[1]
    rows = pattern_ref.shape[0]

    @pl.when(pl.program_id(0) == 0)
    def _():
        row = row_ref[0]
        for d in range(3):
            k = row + d - 1
            inside = jnp.logical_and(k >= 0, k < rows)
            k = jnp.clip(k, 0, rows - 1)
            places = [place_of(pattern_ref, k, t) for t in range(slots)]
            for s in range(slots):
                want = pattern_ref[row, s]
                at = jnp.int32(-1)
                for t in range(slots):
                    at = jnp.where(jnp.logical_and(inside, pattern_ref[k, t] == want), places[t], at)
                at_ref[d, s] = at

    w = w_ref[...]
    for l in range(out_ref.shape[0]):
        cols = []
        for s in range(slots):
            blocks = []
            for d, (low, high) in enumerate(pairs):
                at = at_ref[d, s]
                one = low[l, jnp.clip(at - 1 if d == 0 else at, 0, low.shape[1] - 1)]
                two = high[l, jnp.clip(at - CUT, 0, high.shape[1] - 1)]
                got = jnp.where(at < CUT, one, two)
                blocks.append(got if d == 1 else jnp.where(at >= 0, got, jnp.zeros_like(got)))
            cols.append(jnp.concatenate(blocks, 0))
        res = jnp.dot(w, jnp.concatenate(cols, 1), preferred_element_type=jnp.float32)
        for s in range(slots):
            out_ref[l, s] = res[:, s * 128 : (s + 1) * 128].astype(jnp.bfloat16)


def screen(row, pattern, weights, up, own, down):
    step = 4
    smem = pl.BlockSpec(memory_space=pltpu.SMEM)
    arrays = [*up, *own, *down]
    blocks = [pl.BlockSpec((step, *a.shape[1:]), lambda i: (i, 0, 0, 0)) for a in arrays]
    el, _, bi, wide = own[0].shape
    slots = own[0].shape[1] + own[1].shape[1]
    return pl.pallas_call(
        screen_kernel,
        grid=(el // step,),
        out_shape=jax.ShapeDtypeStruct((el, slots, bi, wide), jnp.bfloat16),
        in_specs=[smem, smem, pl.BlockSpec(weights.shape, lambda i: (0, 0)), *blocks],
        out_specs=pl.BlockSpec((step, slots, bi, wide), lambda i: (i, 0, 0, 0)),
        scratch_shapes=[pltpu.SMEM((3, 5), jnp.int32)],
        cost_estimate=pl.CostEstimate(
            flops=2 * el * slots * bi * 3 * bi * wide, bytes_accessed=8 * el * slots * bi * wide, transcendentals=0
        ),
        compiler_params=pltpu.CompilerParams(vmem_limit_bytes=12 << 20),
        name="screen",
    )(row, pattern, weights, *arrays)


def shards(g_less, g_greater, coulomb, pattern):
    el, rows, slots, bi, wide = g_less.shape
    iz, s_row = lax.axis_index("z"), lax.axis_index("s")
    z_lo = s_row // 2
    turn = iz + z_lo + 1
    fwd, inv = (jnp.asarray(t) for t in tables())

    def piece_of(arr, j, axis, size):
        q = (turn + 4 - j) % 4
        return lax.dynamic_slice_in_dim(arr, q * size, size, axis)

    c = turn % 4
    rot = jnp.stack([
        jnp.where(c == 0, 1.0, jnp.where(c == 2, -1.0, 0.0)),
        jnp.where(c == 1, 1.0, jnp.where(c == 3, -1.0, 0.0)),
        jnp.where(c % 2 == 0, 1.0, -1.0),
    ]).astype(jnp.float32)
    near = (s_row + jnp.arange(3) - 1 + 4) % 4 // 2
    order = (iz + near[:, None] + 2 + jnp.arange(4)[None, :]) % 4
    pick = (order[:, :, None] == jnp.arange(4)[None, None, :]).astype(jnp.bfloat16)
    weights = jnp.einsum(
        "djq,adqp->adjp", pick, coulomb.reshape(bi, 3, NZ, NP), preferred_element_type=jnp.float32
    ).astype(jnp.bfloat16).reshape(bi, 3 * bi)

    cut = CUT
    both = (g_less.reshape(el, slots, bi, wide), g_greater.reshape(el, slots, bi, wide))
    early, late = prepare((turn % 4).reshape(1), s_row.reshape(1), pattern, *both, cut)
    late = [hop(late[j], STEPS[j]) for j in range(4)]
    late[1], rot = lax.optimization_barrier([late[1], marker(rot, [late[0], late[3]], HEAVY)])
    late = gather(late, 0)
    early = lax.all_to_all(early, PLANE, split_axis=0, concat_axis=0, tiled=True)
    early = after(early, late)
    early = [hop(early[:, j], STEPS[j]) for j in range(4)]
    late = lax.all_to_all(late, PLANE, split_axis=0, concat_axis=0, tiled=True)

    late, rot = lax.optimization_barrier([late, marker(rot, early[1:3], HEAVY)])
    hi = correlate(rot, [late], fwd, inv, False, 0, ROOM_HI)
    early[0] = after(early[0], hi)
    lo = correlate(rot, early, fwd, inv, True, HEAVY, ROOM_LO)

    hi = lax.all_to_all(hi, PLANE, split_axis=0, concat_axis=0, tiled=True)
    lo = gather([hop(p, STEPS[j]) for j, p in enumerate(lo)], 0)
    (hi,) = settle([hop(hi[:, j], STEPS[j]) for j in range(4)], False, HEAVY)
    lo = lax.all_to_all(lo, PLANE, split_axis=0, concat_axis=0, tiled=True)
    lo, lo_up, lo_down = settle([after(lo, hi)], True, 0)
    upward, downward = [(0, 1), (1, 2), (2, 3)], [(1, 0), (2, 1), (3, 2)]
    up_hi, down_hi = lax.ppermute(hi, "s", upward), lax.ppermute(hi, "s", downward)
    lo_up, lo_down = lax.optimization_barrier([lo_up, lo_down, up_hi, down_hi])[:2]
    up_lo, down_lo = lax.ppermute(lo_up, "s", upward), lax.ppermute(lo_down, "s", downward)
    return screen(s_row.reshape(1), pattern, weights, (up_lo, up_hi), (lo, hi), (down_lo, down_hi))[:, None]


def solution(mesh):
    fine = Mesh(mesh.devices.reshape(4, 4, 4, 4), ALL)
    energy = ("z", "y", "x")
    return jax.shard_map(
        shards,
        mesh=fine,
        in_specs=(P(energy, "s"), P(energy, "s"), P("s"), P()),
        out_specs=P(energy, "s"),
        check_vma=False,
    )
```

```python
import functools
import math

import jax
import jax.numpy as jnp
import ml_dtypes
import numpy as np
from jax import lax
from jax.experimental import pallas as pl
from jax.experimental.pallas import tpu as pltpu
from jax.sharding import Mesh, PartitionSpec as P

NE = 1024
QUART = NE // 4
NZ = 4
NP = 16
NL = 16
ALL = ("z", "y", "x", "s")
PLANE = ("y", "x")
CUT = 3
ORDER = (0, 3, 1, 2)
BUF = 2
ROOM_HI, ROOM_LO = 52, 52
HEAVY = 100 * 10**9
STEPS = (3, 1, -1, -3)


def tables():
    e = np.arange(QUART)
    out = []
    for first in range(4):
        t = 4 * np.arange(QUART) + first
        angle = 2.0 * math.pi * ((e[:, None] * t[None, :]) % NE) / NE
        scale = 1.0 / math.sqrt(NE)
        real = (np.cos(angle) * scale).astype(np.float32).astype(ml_dtypes.bfloat16)
        imag = (-np.sin(angle) * scale).astype(np.float32).astype(ml_dtypes.bfloat16)
        out.append((real, imag))
    forward = np.stack([np.concatenate([r.T, i.T]) for r, i in out])
    inverse = np.stack([np.concatenate([r, i]) for r, i in out])
    return forward, inverse


def after(value, other):
    return lax.optimization_barrier([value, other])[0]


def hop(piece, step):
    perm = []
    for z in range(4):
        for yx in range(16):
            for s in range(4):
                to = (2 * z + s // 2 + step) % 8
                perm.append(((z * 16 + yx) * 4 + s, ((to // 2) * 16 + yx) * 4 + (to % 2) * 2 + s % 2))
    return lax.ppermute(piece, ALL, perm)


def times_i(v):
    lane = lax.broadcasted_iota(jnp.int32, v.shape, 1)
    return jnp.where(lane < 64, -1.0, 1.0) * pltpu.roll(v, 64, 1)


def correlate_kernel(slots, pieces, split, rot_ref, *refs):
    in_refs, fwd_ref, inv_ref = refs[:pieces], refs[pieces], refs[pieces + 1]
    n_out = 4 if split else 1
    outs = refs[pieces + 2 : pieces + 2 + n_out]
    x_ref, p_ref, y_ref, z_ref, f_ref, b_ref, sem = refs[pieces + 2 + n_out :]
    loads = [
        [pltpu.make_async_copy(ref.at[t1], held.at[t1], sem.at[k, t1]) for t1 in range(4)]
        for k, (ref, held) in enumerate(((fwd_ref, f_ref), (inv_ref, b_ref)))
    ]
    for t1 in range(4):
        for k in range(2):
            loads[k][t1].start()
    f32, bf16 = jnp.float32, jnp.bfloat16
    left = lax.broadcasted_iota(jnp.int32, (32, 128), 1) < 64

    def fetch(j, which, s, p):
        ref = in_refs[j][p : p + 2, which, s] if pieces == 4 else in_refs[0][p : p + 2, j, which, s]
        return ref.reshape(2 * NL, 128).astype(f32)

    for s in range(slots):
        for which in range(2):
            cols = slice((which * slots + s) * 128, (which * slots + s + 1) * 128)
            for p in range(0, NP, 2):
                rows = slice(p * NL, (p + 2) * NL)
                x0, x1, x2, x3 = (fetch(j, which, s, p) for j in range(4))
                a, b, c, d = x0 + x2, x0 - x2, x1 + x3, times_i(x1 - x3)
                for t1, v in enumerate((a + c, b - d, a - c, b + d)):
                    hi = v.astype(bf16)
                    x_ref[t1, 0, rows, cols] = hi
                    x_ref[t1, 1, rows, cols] = (v - hi.astype(f32)).astype(bf16)

    n = slots * 128
    for t1 in range(4):
        loads[0][t1].wait()
        loads[1][t1].wait()
        table, at = f_ref[t1], t1 % BUF
        y_ref[at] = jnp.dot(table, x_ref[t1, 0], preferred_element_type=f32) + jnp.dot(
            table, x_ref[t1, 1], preferred_element_type=f32
        )
        for s in range(slots):
            own, other = slice(s * 128, (s + 1) * 128), slice(n + s * 128, n + (s + 1) * 128)
            for r in range(0, QUART, 32):
                one, two = slice(r, r + 32), slice(QUART + r, QUART + r + 32)
                le = y_ref[at, one, own] + times_i(y_ref[at, two, own])
                gr = y_ref[at, one, other] + times_i(y_ref[at, two, other])
                m1, m2 = le * gr, le * pltpu.roll(gr, 64, 1)
                p_ref[at, one, own] = (
                    jnp.where(left, m1, m2) + pltpu.roll(jnp.where(left, -m2, m1), 64, 1)
                ).astype(bf16)
        z_ref[t1] = jnp.dot(b_ref[t1], p_ref[at], preferred_element_type=f32)

    ca, cb, cc = rot_ref[0], rot_ref[1], rot_ref[2]
    for s in range(slots):
        cols = slice(s * 128, (s + 1) * 128)
        for p in range(0, NP, 2):
            one = slice(p * NL, (p + 2) * NL)
            two = slice(QUART + p * NL, QUART + (p + 2) * NL)
            z0, z1, z2, z3 = (z_ref[t, one, cols] - times_i(z_ref[t, two, cols]) for t in range(4))
            u2 = cc * z2
            a, b = z0 + u2, z0 - u2
            plus, minus = z1 + z3, times_i(z1 - z3)
            c = ca * plus + cb * minus
            d = ca * minus - cb * plus
            for j, v in enumerate((a + c, b - d, a - c, b + d)):
                v = v.astype(bf16).reshape(2, NL, 128)
                if split:
                    outs[j][p : p + 2, s] = v
                else:
                    outs[0][p : p + 2, j, s] = v


def correlate(rot, inputs, fwd, inv, split, flops, room):
    slots = inputs[0].shape[-3]
    n = slots * 128
    vmem = pl.BlockSpec(memory_space=pltpu.VMEM)
    hbm = pl.BlockSpec(memory_space=pltpu.HBM)
    piece = jax.ShapeDtypeStruct((NP, slots, NL, 128), jnp.bfloat16)
    whole = jax.ShapeDtypeStruct((NP, NZ, slots, NL, 128), jnp.bfloat16)
    out = pl.pallas_call(
        functools.partial(correlate_kernel, slots, len(inputs), split),
        out_shape=[piece] * 4 if split else [whole],
        in_specs=[pl.BlockSpec(memory_space=pltpu.SMEM)] + [vmem] * len(inputs) + [hbm] * 2,
        out_specs=[vmem] * (4 if split else 1),
        scratch_shapes=[
            pltpu.VMEM((4, 2, QUART, 2 * n), jnp.bfloat16),
            pltpu.VMEM((BUF, QUART, n), jnp.bfloat16),
            pltpu.VMEM((BUF, 2 * QUART, 2 * n), jnp.float32),
            pltpu.VMEM((4, 2 * QUART, n), jnp.float32),
            pltpu.VMEM((4, 2 * QUART, QUART), jnp.bfloat16),
            pltpu.VMEM((4, 2 * QUART, QUART), jnp.bfloat16),
            pltpu.SemaphoreType.DMA((2, 4)),
        ],
        compiler_params=pltpu.CompilerParams(vmem_limit_bytes=room << 20),
        cost_estimate=pl.CostEstimate(
            flops=flops, bytes_accessed=3 * NE * n * 2 + (2 << 20), transcendentals=0
        ),
        name="correlate",
    )(rot, *inputs, fwd, inv)
    return out if split else out[0]


def turning():
    row = lax.broadcasted_iota(jnp.int32, (256, 256), 0)
    col = lax.broadcasted_iota(jnp.int32, (256, 256), 1)
    return jnp.where((row % 16) * 16 + row // 16 == col, 1.0, 0.0).astype(jnp.bfloat16)


def place_of(pattern_ref, row, slot):
    def plain(t):
        offset = pattern_ref[row, t] - row
        return jnp.logical_and(offset != 0, offset != 6)

    rank = jnp.int32(0)
    for t in range(slot):
        rank = rank + jnp.where(plain(t), 1, 0)
    other = jnp.where(rank == 0, 1, rank + 2)
    return jnp.where(plain(slot), other, jnp.where(pattern_ref[row, slot] == row, 0, 2))


def prepare_kernel(cut, turn_ref, row_ref, pattern_ref, less_ref, great_ref, *refs):
    early_ref, late_refs, turn, held, sem = refs[0], refs[1:5], refs[5], refs[6], refs[7]
    slots = less_ref.shape[1]
    places = [place_of(pattern_ref, row_ref[0], t) for t in range(slots)]
    source = []
    for s in range(slots):
        at = jnp.int32(0)
        for t in range(slots):
            at = jnp.where(places[t] == s, t, at)
        source.append(at)
    loads = [
        [pltpu.make_async_copy(ref.at[:, source[s]], held.at[s, k], sem.at[s, k]) for k, ref in enumerate((less_ref, great_ref))]
        for s in range(slots)
    ]
    order = [*range(cut, slots), *range(cut)]
    for s in order:
        for load in loads[s]:
            load.start()
    turn[...] = turning()
    for s in order:
        for load in loads[s]:
            load.wait()
        for j in range(4):
            q = lax.rem(turn_ref[0] + 4 - j, 4)
            at = pl.ds(pl.multiple_of(q * NP, NP), NP)
            x = jnp.concatenate([held[s, k, :, at, :].reshape(256, 128) for k in range(2)], 1)
            x = jnp.dot(turn[...], x, preferred_element_type=jnp.float32).astype(jnp.bfloat16)
            for k in range(2):
                v = x[:, k * 128 : (k + 1) * 128].reshape(NP, NL, 128)
                if s < cut:
                    early_ref[:, j, k, s] = v
                else:
                    late_refs[j][:, k, s - cut] = v


def prepare(turn, row, pattern, less, great, cut):
    el, slots, bi, wide = less.shape
    vmem = pl.BlockSpec(memory_space=pltpu.VMEM)
    hbm = pl.BlockSpec(memory_space=pltpu.HBM)
    piece = jax.ShapeDtypeStruct((NP, 2, slots - cut, el, wide), jnp.bfloat16)
    early, *late = pl.pallas_call(
        functools.partial(prepare_kernel, cut),
        out_shape=[jax.ShapeDtypeStruct((NP, NZ, 2, cut, el, wide), jnp.bfloat16)] + [piece] * 4,
        in_specs=[pl.BlockSpec(memory_space=pltpu.SMEM)] * 3 + [hbm, hbm],
        out_specs=[vmem] * 5,
        scratch_shapes=[
            pltpu.VMEM((256, 256), jnp.bfloat16),
            pltpu.VMEM((slots, 2, el, bi, wide), jnp.bfloat16),
            pltpu.SemaphoreType.DMA((slots, 2)),
        ],
        compiler_params=pltpu.CompilerParams(vmem_limit_bytes=60 << 20),
        cost_estimate=pl.CostEstimate(flops=0, bytes_accessed=4 * el * slots * bi * wide * 2, transcendentals=0),
        name="prepare",
    )(turn, row, pattern, less, great)
    return early, late


def settle_kernel(slots, pieces, *refs):
    in_refs, out_refs, turn = refs[:pieces], refs[pieces:-1], refs[-1]
    turn[...] = turning()
    for k, j in enumerate(ORDER[::-1]):
        x = [(in_refs[k][:, s] if pieces == 4 else in_refs[0][:, j, s]).reshape(256, 128) for s in range(slots)]
        x = jnp.dot(turn[...], jnp.concatenate(x, 1), preferred_element_type=jnp.float32).astype(jnp.bfloat16)
        for s in range(slots):
            v = x[:, s * 128 : (s + 1) * 128].reshape(NL, NP, 128)
            for out_ref, first in zip(out_refs, (0, 1, 0)):
                if 0 <= s - first < out_ref.shape[1]:
                    out_ref[:, s - first, j * NP : (j + 1) * NP] = v


def settle(inputs, parts, flops):
    slots = inputs[0].shape[-3]
    vmem = pl.BlockSpec(memory_space=pltpu.VMEM)
    counts = [slots, slots - 1, slots - 1] if parts else [slots]
    return pl.pallas_call(
        functools.partial(settle_kernel, slots, len(inputs)),
        out_shape=[jax.ShapeDtypeStruct((NL, n, 64, 128), jnp.bfloat16) for n in counts],
        in_specs=[vmem] * len(inputs),
        out_specs=[vmem] * len(counts),
        scratch_shapes=[pltpu.VMEM((256, 256), jnp.bfloat16)],
        cost_estimate=pl.CostEstimate(flops=flops, bytes_accessed=NL * slots * 64 * 128 * 4, transcendentals=0),
        compiler_params=pltpu.CompilerParams(vmem_limit_bytes=12 << 20),
        name="settle",
    )(*((inputs[j] for j in ORDER[::-1]) if len(inputs) == 4 else inputs))


def gather_kernel(*refs):
    for k, j in enumerate(ORDER):
        refs[4][:, j] = refs[k][...]


def gather(pieces, flops):
    shape = pieces[0].shape
    vmem = pl.BlockSpec(memory_space=pltpu.VMEM)
    return pl.pallas_call(
        gather_kernel,
        out_shape=jax.ShapeDtypeStruct((shape[0], 4, *shape[1:]), jnp.bfloat16),
        in_specs=[vmem] * 4,
        out_specs=vmem,
        cost_estimate=pl.CostEstimate(flops=flops, bytes_accessed=8 * pieces[0].size * 2, transcendentals=0),
        compiler_params=pltpu.CompilerParams(vmem_limit_bytes=12 << 20),
        name="gather",
    )(*(pieces[j] for j in ORDER))


def split_kernel(in_ref, *out_refs):
    for j in range(4):
        out_refs[j][...] = in_ref[:, j]


def split(value):
    shape = value.shape
    rest = shape[2:]
    zeros = (0,) * len(rest)
    return pl.pallas_call(
        split_kernel,
        grid=(4,),
        out_shape=[jax.ShapeDtypeStruct((shape[0], *rest), value.dtype)] * 4,
        in_specs=[pl.BlockSpec((shape[0] // 4, 4, *rest), lambda i: (i, 0, *zeros))],
        out_specs=[pl.BlockSpec((shape[0] // 4, *rest), lambda i: (i, *zeros))] * 4,
        cost_estimate=pl.CostEstimate(flops=0, bytes_accessed=value.size * 4, transcendentals=0),
        compiler_params=pltpu.CompilerParams(vmem_limit_bytes=12 << 20),
        name="split",
    )(value)


def marker(value, pieces, flops):
    hbm = pl.BlockSpec(memory_space=pl.ANY)

    def kernel(*refs):
        refs[-1][...] = refs[0][...]

    return pl.pallas_call(
        kernel,
        out_shape=jax.ShapeDtypeStruct(value.shape, value.dtype),
        in_specs=[pl.BlockSpec(memory_space=pltpu.VMEM)] + [hbm] * len(pieces),
        out_specs=pl.BlockSpec(memory_space=pltpu.VMEM),
        cost_estimate=pl.CostEstimate(flops=flops, bytes_accessed=4096, transcendentals=0),
        compiler_params=pltpu.CompilerParams(vmem_limit_bytes=1 << 20),
        name="marker",
    )(value, *pieces)


def screen_kernel(row_ref, pattern_ref, w_ref, *refs):
    pairs, out_ref, at_ref = (refs[0:2], refs[2:4], refs[4:6]), refs[6], refs[7]
    slots = out_ref.shape[1]
    rows = pattern_ref.shape[0]

    @pl.when(pl.program_id(0) == 0)
    def _():
        row = row_ref[0]
        for d in (1, 0, 2):
            k = row + d - 1
            inside = jnp.logical_and(k >= 0, k < rows)
            k = jnp.clip(k, 0, rows - 1)
            places = [place_of(pattern_ref, k, t) for t in range(slots)]
            for s in range(slots):
                at = jnp.int32(-1)
                for t in range(slots):
                    if d == 1:
                        at = jnp.where(places[t] == s, t, at)
                    else:
                        same = pattern_ref[k, t] == pattern_ref[row, at_ref[1, s]]
                        at = jnp.where(jnp.logical_and(inside, same), places[t], at)
                at_ref[d, s] = at

    w = w_ref[...]
    for l in range(out_ref.shape[0]):
        cols = []
        for s in range(slots):
            blocks = []
            for d, (low, high) in enumerate(pairs):
                if d == 1:
                    blocks.append(low[l, s] if s < CUT else high[l, s - CUT])
                    continue
                at = at_ref[d, s]
                one = low[l, jnp.clip(at - 1 if d == 0 else at, 0, low.shape[1] - 1)]
                two = high[l, jnp.clip(at - CUT, 0, high.shape[1] - 1)]
                got = jnp.where(at < CUT, one, two)
                blocks.append(jnp.where(at >= 0, got, jnp.zeros_like(got)))
            cols.append(jnp.concatenate(blocks, 0))
        res = jnp.dot(w, jnp.concatenate(cols, 1), preferred_element_type=jnp.float32)
        for s in range(slots):
            out_ref[l, at_ref[1, s]] = res[:, s * 128 : (s + 1) * 128].astype(jnp.bfloat16)


def screen(row, pattern, weights, up, own, down):
    step = 4
    smem = pl.BlockSpec(memory_space=pltpu.SMEM)
    arrays = [*up, *own, *down]
    blocks = [pl.BlockSpec((step, *a.shape[1:]), lambda i: (i, 0, 0, 0)) for a in arrays]
    el, _, bi, wide = own[0].shape
    slots = own[0].shape[1] + own[1].shape[1]
    return pl.pallas_call(
        screen_kernel,
        grid=(el // step,),
        out_shape=jax.ShapeDtypeStruct((el, slots, bi, wide), jnp.bfloat16),
        in_specs=[smem, smem, pl.BlockSpec(weights.shape, lambda i: (0, 0)), *blocks],
        out_specs=pl.BlockSpec((step, slots, bi, wide), lambda i: (i, 0, 0, 0)),
        scratch_shapes=[pltpu.SMEM((3, 5), jnp.int32)],
        cost_estimate=pl.CostEstimate(
            flops=2 * el * slots * bi * 3 * bi * wide, bytes_accessed=8 * el * slots * bi * wide, transcendentals=0
        ),
        compiler_params=pltpu.CompilerParams(vmem_limit_bytes=12 << 20),
        name="screen",
    )(row, pattern, weights, *arrays)


def shards(g_less, g_greater, coulomb, pattern):
    el, rows, slots, bi, wide = g_less.shape
    iz, s_row = lax.axis_index("z"), lax.axis_index("s")
    z_lo = s_row // 2
    turn = iz + z_lo + 1
    fwd, inv = (jnp.asarray(t) for t in tables())

    def piece_of(arr, j, axis, size):
        q = (turn + 4 - j) % 4
        return lax.dynamic_slice_in_dim(arr, q * size, size, axis)

    c = turn % 4
    rot = jnp.stack([
        jnp.where(c == 0, 1.0, jnp.where(c == 2, -1.0, 0.0)),
        jnp.where(c == 1, 1.0, jnp.where(c == 3, -1.0, 0.0)),
        jnp.where(c % 2 == 0, 1.0, -1.0),
    ]).astype(jnp.float32)
    near = (s_row + jnp.arange(3) - 1 + 4) % 4 // 2
    order = (iz + near[:, None] + 2 + jnp.arange(4)[None, :]) % 4
    pick = (order[:, :, None] == jnp.arange(4)[None, None, :]).astype(jnp.bfloat16)
    weights = jnp.einsum(
        "djq,adqp->adjp", pick, coulomb.reshape(bi, 3, NZ, NP), preferred_element_type=jnp.float32
    ).astype(jnp.bfloat16).reshape(bi, 3 * bi)

    cut = CUT
    both = (g_less.reshape(el, slots, bi, wide), g_greater.reshape(el, slots, bi, wide))
    early, late = prepare((turn % 4).reshape(1), s_row.reshape(1), pattern, *both, cut)
    late = [hop(late[j], STEPS[j]) for j in range(4)]
    late[1], rot = lax.optimization_barrier([late[1], marker(rot, [late[0], late[3]], HEAVY)])
    late = gather(late, 0)
    early = lax.all_to_all(early, PLANE, split_axis=0, concat_axis=0, tiled=True)
    early = after(early, late)
    early = [hop(p, STEPS[j]) for j, p in enumerate(split(early))]
    late = lax.all_to_all(late, PLANE, split_axis=0, concat_axis=0, tiled=True)

    late, rot = lax.optimization_barrier([late, marker(rot, early[1:3], HEAVY)])
    hi = correlate(rot, [late], fwd, inv, False, 0, ROOM_HI)
    early[0] = after(early[0], hi)
    lo = correlate(rot, early, fwd, inv, True, HEAVY, ROOM_LO)

    hi = lax.all_to_all(hi, PLANE, split_axis=0, concat_axis=0, tiled=True)
    lo = gather([hop(p, STEPS[j]) for j, p in enumerate(lo)], 0)
    (hi,) = settle([hop(hi[:, j], STEPS[j]) for j in range(4)], False, HEAVY)
    lo = lax.all_to_all(lo, PLANE, split_axis=0, concat_axis=0, tiled=True)
    lo, lo_up, lo_down = settle([after(lo, hi)], True, 0)
    upward, downward = [(0, 1), (1, 2), (2, 3)], [(1, 0), (2, 1), (3, 2)]
    up_hi, down_hi = lax.ppermute(hi, "s", upward), lax.ppermute(hi, "s", downward)
    lo_up, lo_down = lax.optimization_barrier([lo_up, lo_down, up_hi, down_hi])[:2]
    up_lo, down_lo = lax.ppermute(lo_up, "s", upward), lax.ppermute(lo_down, "s", downward)
    return screen(s_row.reshape(1), pattern, weights, (up_lo, up_hi), (lo, hi), (down_lo, down_hi))[:, None]


def solution(mesh):
    fine = Mesh(mesh.devices.reshape(4, 4, 4, 4), ALL)
    energy = ("z", "y", "x")
    return jax.shard_map(
        shards,
        mesh=fine,
        in_specs=(P(energy, "s"), P(energy, "s"), P("s"), P()),
        out_specs=P(energy, "s"),
        check_vma=False,
    )
```

```python
import functools
import math

import jax
import jax.numpy as jnp
import ml_dtypes
import numpy as np
from jax import lax
from jax.experimental import pallas as pl
from jax.experimental.pallas import tpu as pltpu
from jax.sharding import Mesh, PartitionSpec as P

NE = 1024
QUART = NE // 4
NZ = 4
NP = 16
NL = 16
ALL = ("z", "y", "x", "s")
PLANE = ("y", "x")
CUT = 3
ORDER = (0, 3, 1, 2)
BUF = 2
ROOM_HI, ROOM_LO = 52, 52
HEAVY = 100 * 10**9
STEPS = (3, 1, -1, -3)


def tables():
    e = np.arange(QUART)
    out = []
    for first in range(4):
        t = 4 * np.arange(QUART) + first
        angle = 2.0 * math.pi * ((e[:, None] * t[None, :]) % NE) / NE
        scale = 1.0 / math.sqrt(NE)
        real = (np.cos(angle) * scale).astype(np.float32).astype(ml_dtypes.bfloat16)
        imag = (-np.sin(angle) * scale).astype(np.float32).astype(ml_dtypes.bfloat16)
        out.append((real, imag))
    forward = np.stack([np.concatenate([r.T, i.T]) for r, i in out])
    inverse = np.stack([np.concatenate([r, i]) for r, i in out])
    return forward, inverse


def after(value, other):
    return lax.optimization_barrier([value, other])[0]


def hop(piece, step):
    perm = []
    for z in range(4):
        for yx in range(16):
            for s in range(4):
                to = (2 * z + s // 2 + step) % 8
                perm.append(((z * 16 + yx) * 4 + s, ((to // 2) * 16 + yx) * 4 + (to % 2) * 2 + s % 2))
    return lax.ppermute(piece, ALL, perm)


def times_i(v):
    lane = lax.broadcasted_iota(jnp.int32, v.shape, 1)
    return jnp.where(lane < 64, -1.0, 1.0) * pltpu.roll(v, 64, 1)


def correlate_kernel(slots, pieces, split, rot_ref, *refs):
    in_refs, fwd_ref, inv_ref = refs[:pieces], refs[pieces], refs[pieces + 1]
    n_out = 4 if split else 1
    outs = refs[pieces + 2 : pieces + 2 + n_out]
    x_ref, p_ref, y_ref, z_ref, f_ref, b_ref, sem = refs[pieces + 2 + n_out :]
    loads = [
        [pltpu.make_async_copy(ref.at[t1], held.at[t1], sem.at[k, t1]) for t1 in range(4)]
        for k, (ref, held) in enumerate(((fwd_ref, f_ref), (inv_ref, b_ref)))
    ]
    for t1 in range(4):
        for k in range(2):
            loads[k][t1].start()
    f32, bf16 = jnp.float32, jnp.bfloat16
    left = lax.broadcasted_iota(jnp.int32, (32, 128), 1) < 64

    def fetch(j, which, s, p):
        ref = in_refs[j][p : p + 2, which, s] if pieces == 4 else in_refs[0][p : p + 2, j, which, s]
        return ref.reshape(2 * NL, 128).astype(f32)

    for s in range(slots):
        for which in range(2):
            cols = slice((which * slots + s) * 128, (which * slots + s + 1) * 128)
            for p in range(0, NP, 2):
                rows = slice(p * NL, (p + 2) * NL)
                x0, x1, x2, x3 = (fetch(j, which, s, p) for j in range(4))
                a, b, c, d = x0 + x2, x0 - x2, x1 + x3, times_i(x1 - x3)
                for t1, v in enumerate((a + c, b - d, a - c, b + d)):
                    hi = v.astype(bf16)
                    x_ref[t1, 0, rows, cols] = hi
                    x_ref[t1, 1, rows, cols] = (v - hi.astype(f32)).astype(bf16)

    n = slots * 128
    for t1 in range(4):
        loads[0][t1].wait()
        loads[1][t1].wait()
        table, at = f_ref[t1], t1 % BUF
        y_ref[at] = jnp.dot(table, x_ref[t1, 0], preferred_element_type=f32) + jnp.dot(
            table, x_ref[t1, 1], preferred_element_type=f32
        )
        for s in range(slots):
            own, other = slice(s * 128, (s + 1) * 128), slice(n + s * 128, n + (s + 1) * 128)
            for r in range(0, QUART, 32):
                one, two = slice(r, r + 32), slice(QUART + r, QUART + r + 32)
                le = y_ref[at, one, own] + times_i(y_ref[at, two, own])
                gr = y_ref[at, one, other] + times_i(y_ref[at, two, other])
                m1, m2 = le * gr, le * pltpu.roll(gr, 64, 1)
                p_ref[at, one, own] = (
                    jnp.where(left, m1, m2) + pltpu.roll(jnp.where(left, -m2, m1), 64, 1)
                ).astype(bf16)
        z_ref[t1] = jnp.dot(b_ref[t1], p_ref[at], preferred_element_type=f32)

    ca, cb, cc = rot_ref[0], rot_ref[1], rot_ref[2]
    for s in range(slots):
        cols = slice(s * 128, (s + 1) * 128)
        for p in range(0, NP, 2):
            one = slice(p * NL, (p + 2) * NL)
            two = slice(QUART + p * NL, QUART + (p + 2) * NL)
            z0, z1, z2, z3 = (z_ref[t, one, cols] - times_i(z_ref[t, two, cols]) for t in range(4))
            u2 = cc * z2
            a, b = z0 + u2, z0 - u2
            plus, minus = z1 + z3, times_i(z1 - z3)
            c = ca * plus + cb * minus
            d = ca * minus - cb * plus
            for j, v in enumerate((a + c, b - d, a - c, b + d)):
                v = v.astype(bf16).reshape(2, NL, 128)
                if split:
                    outs[j][p : p + 2, s] = v
                else:
                    outs[0][p : p + 2, j, s] = v


def correlate(rot, inputs, fwd, inv, split, flops, room):
    slots = inputs[0].shape[-3]
    n = slots * 128
    vmem = pl.BlockSpec(memory_space=pltpu.VMEM)
    hbm = pl.BlockSpec(memory_space=pltpu.HBM)
    piece = jax.ShapeDtypeStruct((NP, slots, NL, 128), jnp.bfloat16)
    whole = jax.ShapeDtypeStruct((NP, NZ, slots, NL, 128), jnp.bfloat16)
    out = pl.pallas_call(
        functools.partial(correlate_kernel, slots, len(inputs), split),
        out_shape=[piece] * 4 if split else [whole],
        in_specs=[pl.BlockSpec(memory_space=pltpu.SMEM)] + [vmem] * len(inputs) + [hbm] * 2,
        out_specs=[vmem] * (4 if split else 1),
        scratch_shapes=[
            pltpu.VMEM((4, 2, QUART, 2 * n), jnp.bfloat16),
            pltpu.VMEM((BUF, QUART, n), jnp.bfloat16),
            pltpu.VMEM((BUF, 2 * QUART, 2 * n), jnp.float32),
            pltpu.VMEM((4, 2 * QUART, n), jnp.float32),
            pltpu.VMEM((4, 2 * QUART, QUART), jnp.bfloat16),
            pltpu.VMEM((4, 2 * QUART, QUART), jnp.bfloat16),
            pltpu.SemaphoreType.DMA((2, 4)),
        ],
        compiler_params=pltpu.CompilerParams(vmem_limit_bytes=room << 20),
        cost_estimate=pl.CostEstimate(
            flops=flops, bytes_accessed=3 * NE * n * 2 + (2 << 20), transcendentals=0
        ),
        name="correlate",
    )(rot, *inputs, fwd, inv)
    return out if split else out[0]


def turning():
    row = lax.broadcasted_iota(jnp.int32, (256, 256), 0)
    col = lax.broadcasted_iota(jnp.int32, (256, 256), 1)
    return jnp.where((row % 16) * 16 + row // 16 == col, 1.0, 0.0).astype(jnp.bfloat16)


def place_of(pattern_ref, row, slot):
    def plain(t):
        offset = pattern_ref[row, t] - row
        return jnp.logical_and(offset != 0, offset != 6)

    rank = jnp.int32(0)
    for t in range(slot):
        rank = rank + jnp.where(plain(t), 1, 0)
    other = jnp.where(rank == 0, 1, rank + 2)
    return jnp.where(plain(slot), other, jnp.where(pattern_ref[row, slot] == row, 0, 2))


def prepare_kernel(cut, turn_ref, row_ref, pattern_ref, less_ref, great_ref, *refs):
    early_ref, late_refs, turn, held, sem = refs[0], refs[1:5], refs[5], refs[6], refs[7]
    slots = less_ref.shape[1]
    places = [place_of(pattern_ref, row_ref[0], t) for t in range(slots)]
    source = []
    for s in range(slots):
        at = jnp.int32(0)
        for t in range(slots):
            at = jnp.where(places[t] == s, t, at)
        source.append(at)
    loads = [
        [pltpu.make_async_copy(ref.at[:, source[s]], held.at[s, k], sem.at[s, k]) for k, ref in enumerate((less_ref, great_ref))]
        for s in range(slots)
    ]
    order = [*range(cut, slots), *range(cut)]
    for s in order:
        for load in loads[s]:
            load.start()
    turn[...] = turning()
    for s in order:
        for load in loads[s]:
            load.wait()
        for j in range(4):
            q = lax.rem(turn_ref[0] + 4 - j, 4)
            at = pl.ds(pl.multiple_of(q * NP, NP), NP)
            x = jnp.concatenate([held[s, k, :, at, :].reshape(256, 128) for k in range(2)], 1)
            x = jnp.dot(turn[...], x, preferred_element_type=jnp.float32).astype(jnp.bfloat16)
            for k in range(2):
                v = x[:, k * 128 : (k + 1) * 128].reshape(NP, NL, 128)
                if s < cut:
                    early_ref[:, j, k, s] = v
                else:
                    late_refs[j][:, k, s - cut] = v


def prepare(turn, row, pattern, less, great, cut):
    el, slots, bi, wide = less.shape
    vmem = pl.BlockSpec(memory_space=pltpu.VMEM)
    hbm = pl.BlockSpec(memory_space=pltpu.HBM)
    piece = jax.ShapeDtypeStruct((NP, 2, slots - cut, el, wide), jnp.bfloat16)
    early, *late = pl.pallas_call(
        functools.partial(prepare_kernel, cut),
        out_shape=[jax.ShapeDtypeStruct((NP, NZ, 2, cut, el, wide), jnp.bfloat16)] + [piece] * 4,
        in_specs=[pl.BlockSpec(memory_space=pltpu.SMEM)] * 3 + [hbm, hbm],
        out_specs=[vmem] * 5,
        scratch_shapes=[
            pltpu.VMEM((256, 256), jnp.bfloat16),
            pltpu.VMEM((slots, 2, el, bi, wide), jnp.bfloat16),
            pltpu.SemaphoreType.DMA((slots, 2)),
        ],
        compiler_params=pltpu.CompilerParams(vmem_limit_bytes=60 << 20),
        cost_estimate=pl.CostEstimate(flops=0, bytes_accessed=4 * el * slots * bi * wide * 2, transcendentals=0),
        name="prepare",
    )(turn, row, pattern, less, great)
    return early, late


def settle_kernel(slots, pieces, *refs):
    in_refs, out_refs, turn = refs[:pieces], refs[pieces:-1], refs[-1]
    turn[...] = turning()
    for k, j in enumerate(ORDER[::-1]):
        x = [(in_refs[k][:, s] if pieces == 4 else in_refs[0][:, j, s]).reshape(256, 128) for s in range(slots)]
        x = jnp.dot(turn[...], jnp.concatenate(x, 1), preferred_element_type=jnp.float32).astype(jnp.bfloat16)
        for s in range(slots):
            v = x[:, s * 128 : (s + 1) * 128].reshape(NL, NP, 128)
            for out_ref, first in zip(out_refs, (0, 1, 0)):
                if 0 <= s - first < out_ref.shape[1]:
                    out_ref[:, s - first, j * NP : (j + 1) * NP] = v


def settle(inputs, parts, flops):
    slots = inputs[0].shape[-3]
    vmem = pl.BlockSpec(memory_space=pltpu.VMEM)
    counts = [slots, slots - 1, slots - 1] if parts else [slots]
    return pl.pallas_call(
        functools.partial(settle_kernel, slots, len(inputs)),
        out_shape=[jax.ShapeDtypeStruct((NL, n, 64, 128), jnp.bfloat16) for n in counts],
        in_specs=[vmem] * len(inputs),
        out_specs=[vmem] * len(counts),
        scratch_shapes=[pltpu.VMEM((256, 256), jnp.bfloat16)],
        cost_estimate=pl.CostEstimate(flops=flops, bytes_accessed=NL * slots * 64 * 128 * 4, transcendentals=0),
        compiler_params=pltpu.CompilerParams(vmem_limit_bytes=12 << 20),
        name="settle",
    )(*((inputs[j] for j in ORDER[::-1]) if len(inputs) == 4 else inputs))


def gather_kernel(*refs):
    for k, j in enumerate(ORDER):
        refs[4][:, j] = refs[k][...]


def gather(pieces, flops):
    shape = pieces[0].shape
    vmem = pl.BlockSpec(memory_space=pltpu.VMEM)
    return pl.pallas_call(
        gather_kernel,
        out_shape=jax.ShapeDtypeStruct((shape[0], 4, *shape[1:]), jnp.bfloat16),
        in_specs=[vmem] * 4,
        out_specs=vmem,
        cost_estimate=pl.CostEstimate(flops=flops, bytes_accessed=8 * pieces[0].size * 2, transcendentals=0),
        compiler_params=pltpu.CompilerParams(vmem_limit_bytes=12 << 20),
        name="gather",
    )(*(pieces[j] for j in ORDER))


def marker(value, pieces, flops):
    hbm = pl.BlockSpec(memory_space=pl.ANY)

    def kernel(*refs):
        refs[-1][...] = refs[0][...]

    return pl.pallas_call(
        kernel,
        out_shape=jax.ShapeDtypeStruct(value.shape, value.dtype),
        in_specs=[pl.BlockSpec(memory_space=pltpu.VMEM)] + [hbm] * len(pieces),
        out_specs=pl.BlockSpec(memory_space=pltpu.VMEM),
        cost_estimate=pl.CostEstimate(flops=flops, bytes_accessed=4096, transcendentals=0),
        compiler_params=pltpu.CompilerParams(vmem_limit_bytes=1 << 20),
        name="marker",
    )(value, *pieces)


def screen_kernel(row_ref, pattern_ref, w_ref, *refs):
    pairs, out_ref, at_ref = (refs[0:2], refs[2:4], refs[4:6]), refs[6], refs[7]
    slots = out_ref.shape[1]
    rows = pattern_ref.shape[0]

    @pl.when(pl.program_id(0) == 0)
    def _():
        row = row_ref[0]
        for d in (1, 0, 2):
            k = row + d - 1
            inside = jnp.logical_and(k >= 0, k < rows)
            k = jnp.clip(k, 0, rows - 1)
            places = [place_of(pattern_ref, k, t) for t in range(slots)]
            for s in range(slots):
                at = jnp.int32(-1)
                for t in range(slots):
                    if d == 1:
                        at = jnp.where(places[t] == s, t, at)
                    else:
                        same = pattern_ref[k, t] == pattern_ref[row, at_ref[1, s]]
                        at = jnp.where(jnp.logical_and(inside, same), places[t], at)
                at_ref[d, s] = at

    w = w_ref[...]
    for l in range(out_ref.shape[0]):
        cols = []
        for s in range(slots):
            blocks = []
            for d, (low, high) in enumerate(pairs):
                if d == 1:
                    blocks.append(low[l, s] if s < CUT else high[l, s - CUT])
                    continue
                at = at_ref[d, s]
                one = low[l, jnp.clip(at - 1 if d == 0 else at, 0, low.shape[1] - 1)]
                two = high[l, jnp.clip(at - CUT, 0, high.shape[1] - 1)]
                got = jnp.where(at < CUT, one, two)
                blocks.append(jnp.where(at >= 0, got, jnp.zeros_like(got)))
            cols.append(jnp.concatenate(blocks, 0))
        res = jnp.dot(w, jnp.concatenate(cols, 1), preferred_element_type=jnp.float32)
        for s in range(slots):
            out_ref[l, at_ref[1, s]] = res[:, s * 128 : (s + 1) * 128].astype(jnp.bfloat16)


def screen(row, pattern, weights, up, own, down):
    step = 4
    smem = pl.BlockSpec(memory_space=pltpu.SMEM)
    arrays = [*up, *own, *down]
    blocks = [pl.BlockSpec((step, *a.shape[1:]), lambda i: (i, 0, 0, 0)) for a in arrays]
    el, _, bi, wide = own[0].shape
    slots = own[0].shape[1] + own[1].shape[1]
    return pl.pallas_call(
        screen_kernel,
        grid=(el // step,),
        out_shape=jax.ShapeDtypeStruct((el, slots, bi, wide), jnp.bfloat16),
        in_specs=[smem, smem, pl.BlockSpec(weights.shape, lambda i: (0, 0)), *blocks],
        out_specs=pl.BlockSpec((step, slots, bi, wide), lambda i: (i, 0, 0, 0)),
        scratch_shapes=[pltpu.SMEM((3, 5), jnp.int32)],
        cost_estimate=pl.CostEstimate(
            flops=2 * el * slots * bi * 3 * bi * wide, bytes_accessed=8 * el * slots * bi * wide, transcendentals=0
        ),
        compiler_params=pltpu.CompilerParams(vmem_limit_bytes=12 << 20),
        name="screen",
    )(row, pattern, weights, *arrays)


def shards(g_less, g_greater, coulomb, pattern):
    el, rows, slots, bi, wide = g_less.shape
    iz, s_row = lax.axis_index("z"), lax.axis_index("s")
    z_lo = s_row // 2
    turn = iz + z_lo + 1
    fwd, inv = (jnp.asarray(t) for t in tables())

    def piece_of(arr, j, axis, size):
        q = (turn + 4 - j) % 4
        return lax.dynamic_slice_in_dim(arr, q * size, size, axis)

    c = turn % 4
    rot = jnp.stack([
        jnp.where(c == 0, 1.0, jnp.where(c == 2, -1.0, 0.0)),
        jnp.where(c == 1, 1.0, jnp.where(c == 3, -1.0, 0.0)),
        jnp.where(c % 2 == 0, 1.0, -1.0),
    ]).astype(jnp.float32)
    near = (s_row + jnp.arange(3) - 1 + 4) % 4 // 2
    order = (iz + near[:, None] + 2 + jnp.arange(4)[None, :]) % 4
    pick = (order[:, :, None] == jnp.arange(4)[None, None, :]).astype(jnp.bfloat16)
    weights = jnp.einsum(
        "djq,adqp->adjp", pick, coulomb.reshape(bi, 3, NZ, NP), preferred_element_type=jnp.float32
    ).astype(jnp.bfloat16).reshape(bi, 3 * bi)

    cut = CUT
    both = (g_less.reshape(el, slots, bi, wide), g_greater.reshape(el, slots, bi, wide))
    early, late = prepare((turn % 4).reshape(1), s_row.reshape(1), pattern, *both, cut)
    late = [hop(late[j], STEPS[j]) for j in range(4)]
    late[1], rot = lax.optimization_barrier([late[1], marker(rot, [late[0], late[3]], HEAVY)])
    late = gather(late, 0)
    early = lax.all_to_all(early, PLANE, split_axis=0, concat_axis=0, tiled=True)
    early = after(early, late)
    early = [hop(early[:, j], STEPS[j]) for j in range(4)]
    late = lax.all_to_all(late, PLANE, split_axis=0, concat_axis=0, tiled=True)

    late, rot = lax.optimization_barrier([late, marker(rot, early[1:3], HEAVY)])
    hi = correlate(rot, [late], fwd, inv, False, 0, ROOM_HI)
    early[0] = after(early[0], hi)
    lo = correlate(rot, early, fwd, inv, True, HEAVY, ROOM_LO)

    hi = lax.all_to_all(hi, PLANE, split_axis=0, concat_axis=0, tiled=True)
    lo = gather([hop(p, STEPS[j]) for j, p in enumerate(lo)], 0)
    (hi,) = settle([hop(hi[:, j], STEPS[j]) for j in range(4)], False, HEAVY)
    lo = lax.all_to_all(lo, PLANE, split_axis=0, concat_axis=0, tiled=True)
    lo, lo_up, lo_down = settle([after(lo, hi)], True, 0)
    upward, downward = [(0, 1), (1, 2), (2, 3)], [(1, 0), (2, 1), (3, 2)]
    up_hi, down_hi = lax.ppermute(hi, "s", upward), lax.ppermute(hi, "s", downward)
    lo_up, lo_down = lax.optimization_barrier([lo_up, lo_down, up_hi, down_hi])[:2]
    up_lo, down_lo = lax.ppermute(lo_up, "s", upward), lax.ppermute(lo_down, "s", downward)
    return screen(s_row.reshape(1), pattern, weights, (up_lo, up_hi), (lo, hi), (down_lo, down_hi))[:, None]


def solution(mesh):
    fine = Mesh(mesh.devices.reshape(4, 4, 4, 4), ALL)
    energy = ("z", "y", "x")
    return jax.shard_map(
        shards,
        mesh=fine,
        in_specs=(P(energy, "s"), P(energy, "s"), P("s"), P()),
        out_specs=P(energy, "s"),
        check_vma=False,
    )
```
